512 devices in a mesh: clus: 64 (over x, z, core), coef: 8 (over y).
Axes of the slice: x: 4, y: 8, z: 8, core: 2. Of those that a mesh axis runs over, the one named last changes fastest.
Arguments:
- density: bfloat16 [1024, 128, 256], P('clus', 'coef'), may hold values from -6 to 6
- near_list: int32 [1024, 9], P('clus'), may hold values from 0 to 1023, as said below
- far_list: int32 [128, 27], P('clus'), may hold values from 0 to 127
- near_blocks: bfloat16 [1024, 9, 128, 128], P('clus', None, 'coef'), may hold values from -0.1875 to 0.1875
- basis: bfloat16 [1024, 128, 64], P('clus', 'coef'), may hold values from -0.5 to 0.5
- transfer: bfloat16 [1024, 64, 64], P('clus'), may hold values from -0.25 to 0.25
- coupling: bfloat16 [128, 27, 64, 64], P('clus', None, None, 'coef'), may hold values from -0.15625 to 0.15625
Outputs:
- first: bfloat16 [1024, 128, 256], P('clus', 'coef')
- second: bfloat16 [1024, 128, 256], P('clus', 'coef')
The draws below stay inside these ranges and needn't reach their ends.
Inputs may be any that keep to these rules, and one draw needn't show every extreme that they name: near_list[i, 0] is i itself; every entry differs from its row's cluster i by at most 4, and entries i + 4 and i - 4 appear wherever they lie in range.
All inputs are finite; a program needn't handle non-finite values.
Results may differ from the reference program's by a relative error of at most 0.014.
Values may be sent and summed in bfloat16 or wider, within the bound.
No kernel may reach another device: no remote copies, remote signals or barrier semaphores. Data moves between devices by JAX's collectives and lax.ppermute only.
A program may use at most 64 MiB of HBM per device.

```python
import jax
import jax.numpy as jnp
from jax import lax

PANEL = 128
RANK = 64
NRHS = 256
CHILD = 8
NEAR_K = 9
FAR_K = 27
NWIN = 4
CLUSTERS = 1024
PARENTS = 128


def draw_near_list(key, part):
    rows = jnp.arange(CLUSTERS, dtype=jnp.int32)[:, None]
    shifts = jax.random.randint(key, (CLUSTERS, NEAR_K), -NWIN, NWIN + 1, dtype=jnp.int32)
    column = jnp.arange(NEAR_K, dtype=jnp.int32)[None, :]
    shifts = jnp.where(column == 0, 0, jnp.where(column == 1, NWIN, jnp.where(column == 2, -NWIN, shifts)))
    return jnp.clip(rows + shifts, 0, CLUSTERS - 1).astype(jnp.int32)


def place_ends(array, key, least, top_value):
    longest = array.shape.index(max(array.shape))
    spots = []
    for shift in (0, 1):
        where = [jax.random.randint(jax.random.fold_in(key, axis), (), 0, length) for axis, length in enumerate(array.shape)]
        where[longest] = (where[longest] + shift) % array.shape[longest]
        spots.append(tuple(where))
    return array.at[spots[0]].set(least).at[spots[1]].set(top_value)


def shard_levels(rng, shape, shards, low, high):
    factor_of, own = 1.0, jax.random.fold_in(rng, 6)
    for dim, parts in shards:
        draws = jnp.exp(jax.random.uniform(jax.random.fold_in(own, dim), (parts,), jnp.float32, low / len(shards), high / len(shards)))
        factor_of = factor_of * jnp.repeat(draws, shape[dim] // parts).reshape([-1 if axis == dim else 1 for axis in range(len(shape))])
    return factor_of


def bell_draw(stream_key, shape, spread, reach, pieces=(), held_as=jnp.bfloat16):
    array = spread * jax.random.normal(stream_key, shape, jnp.float32)
    if pieces:
        array = array * shard_levels(stream_key, shape, pieces, -0.22, 0.18)
    return jnp.clip(array, -reach, reach).astype(held_as)


def setup_inputs(seed: int = 0) -> dict:
    splits = jax.random.split(jax.random.key(seed), 8)
    return {
        "density": bell_draw(splits[0], (CLUSTERS, PANEL, NRHS), 1.0, 6.0, ((0, 64), (1, 8))),
        "near_list": draw_near_list(jax.random.fold_in(splits[7], 71), 0),
        "far_list": place_ends(jax.random.randint(splits[2], (PARENTS, FAR_K), 0, PARENTS), jax.random.fold_in(splits[2], 1), 0, PARENTS - 1).astype(jnp.int32),
        "near_blocks": bell_draw(splits[3], (CLUSTERS, NEAR_K, PANEL, PANEL), (NEAR_K * PANEL) ** -0.5, 0.1875, ((0, 64), (2, 8))),
        "basis": bell_draw(splits[4], (CLUSTERS, PANEL, RANK), PANEL ** -0.5, 0.5, ((0, 64), (1, 8))),
        "transfer": bell_draw(splits[5], (CLUSTERS, RANK, RANK), (CHILD * RANK) ** -0.5, 0.25, ((0, 64),)),
        "coupling": bell_draw(splits[6], (PARENTS, FAR_K, RANK, RANK), (FAR_K * RANK) ** -0.5, 0.15625, ((0, 64), (3, 8))),
    }


def apply_operator(values, near_list, far_list, near_blocks, basis, transfer, coupling):
    clusters = values.shape[0]
    parents = clusters // CHILD
    highest = lax.Precision.HIGHEST
    wide = values.astype(jnp.float32)
    base = basis.astype(jnp.float32)
    coeffs = jnp.einsum('ins,inr->isr', base, wide, precision=highest)
    grouped = transfer.astype(jnp.float32).reshape(parents, CHILD, RANK, RANK)
    parent_coef = jnp.einsum('pcsq,pcsr->pqr', grouped, coeffs.reshape(parents, CHILD, RANK, NRHS), precision=highest).astype(jnp.bfloat16)
    picked = jnp.take(parent_coef, far_list.reshape(-1), axis=0).reshape(parents, FAR_K, RANK, NRHS).astype(jnp.float32)
    coupled = jnp.einsum('pkaq,pkqr->par', coupling.astype(jnp.float32), picked, precision=highest).astype(jnp.bfloat16)
    lower = jnp.einsum('pcsq,pqr->pcsr', grouped, coupled.astype(jnp.float32), precision=highest).astype(jnp.bfloat16)
    lower = lower.reshape(clusters, RANK, NRHS).astype(jnp.float32)
    total = jnp.einsum('ins,isr->inr', base, lower, precision=highest)
    for column in range(NEAR_K):
        rows = jnp.take(values, near_list[:, column], axis=0).astype(jnp.float32)
        total = total + jnp.einsum('imn,inr->imr', near_blocks[:, column].astype(jnp.float32), rows, precision=highest)
    return total.astype(jnp.bfloat16)


def reference(density, near_list, far_list, near_blocks, basis, transfer, coupling):
    first = apply_operator(density, near_list, far_list, near_blocks, basis, transfer, coupling)
    second = apply_operator(first, near_list, far_list, near_blocks, basis, transfer, coupling)
    return (first, second)
```

```python
import functools

import jax
import jax.numpy as jnp
from jax import lax
from jax.experimental import pallas as pl
from jax.experimental.pallas import tpu as pltpu
from jax.sharding import Mesh
from jax.sharding import PartitionSpec as P

BF = jnp.bfloat16
F32 = jnp.float32
LEAVES = 16
ROWS = 16
PANEL = 128
RANK = 64
COLS = 32
PACK = 4
GROUPS = LEAVES // PACK
NEAR_K = 9
FAR_K = 27
NWIN = 4
SHARES = 8
PLANE = 32
VEC0 = 0
PAR0 = VEC0 + GROUPS * ROWS
U0 = PAR0 + 32
CPL0 = U0 + LEAVES // 2 * ROWS
SENT = CPL0 + FAR_K * 8
CLUS = ("x", "z", "core")
TOP = (((0,), (0,)), ((), ()))


def dot(a, b):
    return jnp.dot(a, b, preferred_element_type=F32)


def dot_top(a, b):
    return lax.dot_general(a, b, TOP, preferred_element_type=F32)


def lane_group(shape):
    return lax.broadcasted_iota(jnp.int32, shape, len(shape) - 1) // COLS


def spread(rows):
    rows = rows + pltpu.roll(rows, 64, 1)
    return rows + pltpu.roll(rows, 32, 1)


def pack_parents(first, second):
    group = lane_group((32, 128))
    low = jnp.where(group == 0, first[:32], first[32:])
    high = jnp.where(group == 2, second[:32], second[32:])
    return jnp.where(group < 2, low, high).astype(BF)


def prepare_kernel(d_ref, b_ref, t_ref, c_ref, out_ref):
    u = [dot(b_ref[i], t_ref[i]) for i in range(LEAVES)]
    for m in range(LEAVES // 2):
        pair = jnp.concatenate([u[2 * m], u[2 * m + 1]], axis=1).astype(BF)
        for s in range(SHARES):
            out_ref[s, U0 + ROWS * m : U0 + ROWS * (m + 1), :] = pair
    part = []
    for p in range(2):
        rows = jnp.concatenate(u[8 * p : 8 * p + 8], axis=0).astype(BF)
        part.append(dot_top(rows, d_ref[8 * p : 8 * p + 8].reshape(8 * ROWS, 256)))
    for s in range(SHARES):
        cut = slice(COLS * s, COLS * (s + 1))
        pieces = [part[0][:32, cut], part[0][32:, cut], part[1][:32, cut], part[1][32:, cut]]
        out_ref[s, PAR0 : PAR0 + 32, :] = jnp.concatenate(pieces, axis=1).astype(BF)
        for g in range(GROUPS):
            pieces = [d_ref[PACK * g + l][:, cut] for l in range(PACK)]
            out_ref[s, VEC0 + ROWS * g : VEC0 + ROWS * (g + 1), :] = jnp.concatenate(pieces, axis=1)
    both = jnp.concatenate([c_ref[0].astype(F32), c_ref[1].astype(F32)], axis=2)
    both = both.reshape(FAR_K * 8, 128).astype(BF)
    for s in range(SHARES):
        out_ref[s, CPL0:SENT, :] = both


def parent_kernel(recv_ref, out_ref):
    total = jnp.sum(recv_ref[...].astype(F32), axis=0).astype(BF)
    out_ref[...] = jnp.broadcast_to(total[None], out_ref.shape)


def coupled_kernel(far_ref, pc_ref, recv_ref, out_ref, c_scr, rhs_scr):
    for y in range(SHARES):
        rows = recv_ref[y, CPL0:SENT, :].astype(F32).reshape(FAR_K, 8, 128)
        c_scr[:, 8 * y : 8 * y + 8, :] = rows
    low = c_scr[:, :32, :].reshape(FAR_K * 32, 128).astype(BF)
    high = c_scr[:, 32:, :].reshape(FAR_K * 32, 128).astype(BF)
    side = lax.broadcasted_iota(jnp.int32, (32, 128), 1) // 64
    even = lane_group((RANK, 128)) % 2 == 0
    for p in range(2):
        for k in range(FAR_K):
            parent = far_ref[p, k]
            tile = pc_ref[(parent // 2) % 2, parent // 4]
            rhs_scr[32 * k : 32 * (k + 1), :] = jnp.where(side == parent % 2, tile, jnp.zeros_like(tile))
        rhs = rhs_scr[...]
        acc0 = dot_top(low, rhs)[64 * p : 64 * (p + 1)]
        acc1 = dot_top(high, rhs)[64 * p : 64 * (p + 1)]
        out_ref[p] = spread(jnp.where(even, acc0, acc1)).astype(BF)


def apply_kernel(last, near_idx, *refs):
    if last:
        near_ref, vec_ref, lo_ref, hi_ref, u_ref, c_ref, own_ref, out_ref, v_scr = refs
    else:
        near_ref, vec_ref, lo_ref, hi_ref, u_ref, c_ref, out_ref, pc_ref, v_scr, acc_scr = refs
    g = pl.program_id(0)

    @pl.when(g == 0)
    def _():
        for group in range(GROUPS + 2):
            if group == 0:
                tile = lo_ref[...]
            elif group == GROUPS + 1:
                tile = hi_ref[...]
            elif last:
                tile = vec_ref[:, group - 1]
            else:
                tile = vec_ref[:, ROWS * (group - 1) : ROWS * group, :]
            tile = tile.reshape(PANEL, 128)
            for l in range(PACK):
                v_scr[PACK * group + l] = tile[:, COLS * l : COLS * (l + 1)]
        if not last:
            acc_scr[...] = jnp.zeros_like(acc_scr)

    cols = []
    for l in range(PACK):
        i = PACK * g + l
        lhs = jnp.concatenate([near_ref[:, l, k].reshape(PANEL, PANEL) for k in range(NEAR_K)], axis=1)
        rhs = jnp.concatenate([v_scr[near_idx[i, k]] for k in range(NEAR_K)], axis=0)
        cols.append(dot(lhs, rhs))
    base = pl.multiple_of(U0 + 2 * ROWS * g, ROWS)
    u = u_ref[:, pl.ds(base, 2 * ROWS), :]
    u = jnp.concatenate([u[:, :ROWS].reshape(PANEL, 128), u[:, ROWS:].reshape(PANEL, 128)], axis=1)
    coef = c_ref[g // 2].astype(F32)
    group = lane_group((RANK, 128))
    blocks = [jnp.where(group == l, coef, 0.0) for l in range(PACK)]
    far = dot(u, jnp.concatenate(blocks, axis=0).astype(BF))
    res = (jnp.concatenate(cols, axis=1) + far).astype(BF)
    tile = res.reshape(SHARES, ROWS, 128)
    if last:
        out_ref[:, 0, 0] = own_ref[:, 0]
        out_ref[:, 1, 0] = tile
        return
    out_ref[:, 0] = tile
    x = dot_top(u, res)
    y = jnp.zeros((RANK, 128), F32)
    for l in range(PACK):
        y = y + jnp.where(group == l, x[RANK * l : RANK * (l + 1)], 0.0)
    acc_scr[g // 2] = acc_scr[g // 2] + y

    @pl.when(g == GROUPS - 1)
    def _():
        packed = pack_parents(spread(acc_scr[0]), spread(acc_scr[1]))
        pc_ref[...] = jnp.broadcast_to(packed[None], pc_ref.shape)


def finish_kernel(recv_ref, first_ref, second_ref):
    for o, ref in enumerate((first_ref, second_ref)):
        for g in range(GROUPS):
            for b in range(2):
                tiles = [recv_ref[PACK * b + s, o, g] for s in range(PACK)]
                for l in range(PACK):
                    cut = slice(COLS * l, COLS * (l + 1))
                    ref[PACK * g + l, :, 128 * b : 128 * (b + 1)] = jnp.concatenate([t[:, cut] for t in tiles], axis=1)


def vmem(n):
    return [pl.BlockSpec(memory_space=pltpu.VMEM)] * n


def cost(flops, nbytes):
    return pl.CostEstimate(flops=flops, bytes_accessed=nbytes, transcendentals=0)


def prepare(density, basis, transfer, coupling):
    return pl.pallas_call(
        prepare_kernel,
        out_shape=jax.ShapeDtypeStruct((SHARES, SENT, 128), BF),
        in_specs=vmem(4),
        out_specs=vmem(1)[0],
        cost_estimate=cost(40_000_000, 1_500_000),
        name="prepare",
    )(density, basis, transfer, jnp.swapaxes(coupling, 2, 3))


def first_parents(recv):
    return pl.pallas_call(
        parent_kernel,
        grid=(1,),
        out_shape=jax.ShapeDtypeStruct((PLANE, 32, 128), BF),
        in_specs=[pl.BlockSpec((SHARES, 32, 128), lambda i: (0, PAR0 // 32, 0))],
        out_specs=pl.BlockSpec((PLANE, 32, 128), lambda i: (0, 0, 0)),
        cost_estimate=cost(100_000, 350_000),
        name="parents",
    )(recv)


def couple(far_list, every, recv):
    return pl.pallas_call(
        coupled_kernel,
        out_shape=jax.ShapeDtypeStruct((2, RANK, 128), BF),
        in_specs=[pl.BlockSpec(memory_space=pltpu.SMEM)] + vmem(2),
        out_specs=vmem(1)[0],
        scratch_shapes=[pltpu.VMEM((FAR_K, RANK, 128), F32), pltpu.VMEM((FAR_K * 32, 128), BF)],
        cost_estimate=cost(100_000_000, 1_500_000),
        name="couple",
    )(far_list, every, recv)


def apply(near_idx, near, vec, low, high, recv, coef, own=None):
    last = own is not None
    whole = lambda *shape: pl.BlockSpec(shape, lambda g, idx: (0,) * len(shape))
    share = pl.BlockSpec((SHARES, 1, ROWS, 128), lambda g, idx: (0, g, 0, 0))
    in_specs = [
        pl.BlockSpec((SHARES, PACK, NEAR_K, ROWS, PANEL), lambda g, idx: (0, g, 0, 0, 0)),
        whole(SHARES, GROUPS, ROWS, 128) if last else whole(SHARES, SENT, 128),
        whole(SHARES, ROWS, 128),
        whole(SHARES, ROWS, 128),
        whole(SHARES, SENT, 128),
        whole(2, RANK, 128),
    ]
    scratch = [pltpu.VMEM((LEAVES + 2 * NWIN, PANEL, COLS), BF)]
    operands = [near, vec, low, high, recv, coef]
    if last:
        in_specs.append(share)
        operands.append(own)
        out_shape = jax.ShapeDtypeStruct((SHARES, 2, GROUPS, ROWS, 128), BF)
        out_specs = pl.BlockSpec((SHARES, 2, 1, ROWS, 128), lambda g, idx: (0, 0, g, 0, 0))
    else:
        scratch.append(pltpu.VMEM((2, RANK, 128), F32))
        out_shape = (
            jax.ShapeDtypeStruct((SHARES, GROUPS, ROWS, 128), BF),
            jax.ShapeDtypeStruct((PLANE, 32, 128), BF),
        )
        out_specs = (share, whole(PLANE, 32, 128))
    return pl.pallas_call(
        functools.partial(apply_kernel, last),
        grid_spec=pltpu.PrefetchScalarGridSpec(
            num_scalar_prefetch=1,
            grid=(GROUPS,),
            in_specs=in_specs,
            out_specs=out_specs,
            scratch_shapes=scratch,
        ),
        out_shape=out_shape,
        cost_estimate=cost(300_000_000, 6_000_000),
        name="apply_last" if last else "apply_first",
    )(near_idx, *operands)


def finish(recv):
    out = jax.ShapeDtypeStruct((LEAVES, ROWS, 256), BF)
    return pl.pallas_call(
        finish_kernel,
        out_shape=(out, out),
        in_specs=vmem(1),
        out_specs=tuple(vmem(2)),
        cost_estimate=cost(100_000, 600_000),
        name="finish",
    )(recv)


def gather_parents(packed):
    plane = lax.all_to_all(packed, ("x", "z"), 0, 0)
    return lax.all_gather(plane, "core", axis=0)


def halo(bottom, top):
    count = 64
    forward = [(i, i + 1) for i in range(count - 1)]
    backward = [(target, source) for source, target in forward]
    return lax.ppermute(top, CLUS, forward), lax.ppermute(bottom, CLUS, backward)


def body(density, near_list, far_list, near_blocks, basis, transfer, coupling):
    near = lax.all_gather(near_blocks, "y", axis=0)
    near_idx = near_list - (lax.axis_index(CLUS) * LEAVES - NWIN)
    near_idx = jnp.clip(near_idx, 0, LEAVES + 2 * NWIN - 1)
    recv = lax.all_to_all(prepare(density, basis, transfer, coupling), "y", 0, 0)
    every = gather_parents(first_parents(recv))
    low, high = halo(recv[:, :ROWS], recv[:, ROWS * (GROUPS - 1) : ROWS * GROUPS])
    coef = couple(far_list, every, recv)
    first, parents = apply(near_idx, near, recv, low, high, recv, coef)
    low, high = halo(first[:, 0], first[:, GROUPS - 1])
    every = gather_parents(parents)
    coef = couple(far_list, every, recv)
    sent = apply(near_idx, near, first, low, high, recv, coef, own=first)
    return finish(lax.all_to_all(sent, "y", 0, 0))


def solution(mesh):
    fine = Mesh(mesh.devices.reshape(4, 8, 2, 8), ("x", "z", "core", "y"))
    placed = (
        P(CLUS, "y", None),
        P(CLUS, None),
        P(CLUS, None),
        P(CLUS, None, "y", None),
        P(CLUS, "y", None),
        P(CLUS, None, None),
        P(CLUS, None, None, "y"),
    )
    return jax.shard_map(
        body,
        mesh=fine,
        in_specs=placed,
        out_specs=(P(CLUS, "y", None), P(CLUS, "y", None)),
        check_vma=False,
    )
```

```python
import jax
import jax.numpy as jnp
from jax import lax
from jax.experimental import pallas as pl
from jax.experimental.pallas import tpu as pltpu
from jax.sharding import Mesh
from jax.sharding import PartitionSpec as P

BF = jnp.bfloat16
F32 = jnp.float32
LEAVES = 16
ROWS = 16
PANEL = 128
RANK = 64
COLS = 32
PACK = 4
GROUPS = LEAVES // PACK
NEAR_K = 9
FAR_K = 27
NWIN = 4
SHARES = 8
PLANE = 32
PAR0 = GROUPS * ROWS
SENT = PAR0 + 32
BAS0 = LEAVES * NEAR_K * ROWS
CPL0 = BAS0 + LEAVES // 2 * ROWS
HELD = CPL0 + FAR_K * 8
HALF = FAR_K * 32
CLUS = ("x", "z", "core")
TOP = (((0,), (0,)), ((), ()))
ANY = pl.BlockSpec(memory_space=pl.ANY)
SMEM = pl.BlockSpec(memory_space=pltpu.SMEM)
VMEM = pl.BlockSpec(memory_space=pltpu.VMEM)


def dot(a, b):
    return jnp.dot(a, b, preferred_element_type=F32)


def dot_top(a, b):
    return lax.dot_general(a, b, TOP, preferred_element_type=F32)


def lane_group(shape):
    return lax.broadcasted_iota(jnp.int32, shape, len(shape) - 1) // COLS


def spread(rows):
    rows = rows + pltpu.roll(rows, 64, 1)
    return rows + pltpu.roll(rows, 32, 1)


def pack_parents(first, second):
    group = lane_group((32, 128))
    low = jnp.where(group == 0, first[:32], first[32:])
    high = jnp.where(group == 2, second[:32], second[32:])
    return jnp.where(group < 2, low, high).astype(BF)


def stack_kernel(near_ref, b_ref, c_ref, out_ref):
    out_ref[:BAS0] = near_ref[...].reshape(BAS0, PANEL)
    for m in range(LEAVES // 2):
        row = BAS0 + ROWS * m
        out_ref[row : row + ROWS] = jnp.concatenate([b_ref[2 * m], b_ref[2 * m + 1]], axis=1)
    both = jnp.concatenate([c_ref[0].astype(F32), c_ref[1].astype(F32)], axis=2)
    out_ref[CPL0:] = both.reshape(FAR_K * 8, 128).astype(BF)


def prepare_kernel(d_ref, b_ref, t_ref, out_ref):
    part = []
    for p in range(2):
        u = [dot(b_ref[i], t_ref[i]) for i in range(8 * p, 8 * p + 8)]
        rows = jnp.concatenate(u, axis=0).astype(BF)
        part.append(dot_top(rows, d_ref[8 * p : 8 * p + 8].reshape(8 * ROWS, 256)))
    for s in range(SHARES):
        cut = slice(COLS * s, COLS * (s + 1))
        pieces = [part[0][:32, cut], part[0][32:, cut], part[1][:32, cut], part[1][32:, cut]]
        out_ref[s, PAR0:SENT, :] = jnp.concatenate(pieces, axis=1).astype(BF)
        for g in range(GROUPS):
            pieces = [d_ref[PACK * g + l][:, cut] for l in range(PACK)]
            out_ref[s, ROWS * g : ROWS * (g + 1), :] = jnp.concatenate(pieces, axis=1)


def parent_kernel(recv_ref, out_ref, bottom_ref, top_ref):
    total = jnp.sum(recv_ref[:, PAR0:SENT, :].astype(F32), axis=0).astype(BF)
    out_ref[...] = jnp.broadcast_to(total[None], out_ref.shape)
    bottom_ref[...] = recv_ref[:, :ROWS, :]
    top_ref[...] = recv_ref[:, PAR0 - ROWS : PAR0, :]


def far_sums(far_ref, pc_ref, cpl, rhs_scr):
    side = lax.broadcasted_iota(jnp.int32, (32, 128), 1) // 64
    even = lane_group((RANK, 128)) % 2 == 0
    sums = []
    for p in range(2):
        for k in range(FAR_K):
            parent = far_ref[p, k]
            tile = pc_ref[(parent // 2) % 2, parent // 4]
            rhs_scr[32 * k : 32 * (k + 1), :] = jnp.where(side == parent % 2, tile, jnp.zeros_like(tile))
        rhs = rhs_scr[...]
        acc0 = dot(cpl[0][RANK * p : RANK * (p + 1)], rhs)
        acc1 = dot(cpl[1][RANK * p : RANK * (p + 1)], rhs)
        sums.append(spread(jnp.where(even, acc0, acc1)).astype(BF).astype(F32))
    return sums


def far_field(u, coef):
    group = lane_group((RANK, 128))
    blocks = [jnp.where(group == l, coef, 0.0) for l in range(PACK)]
    return dot(u, jnp.concatenate(blocks, axis=0).astype(BF))


def near_copies(w_ref, near_scr, sems):
    size = NEAR_K * ROWS
    return [
        pltpu.make_async_copy(w_ref.at[:, pl.ds(size * i, size), :], near_scr.at[i], sems.at[i])
        for i in range(LEAVES)
    ]


def unpack(tiles, v_scr):
    for n, tile in enumerate(tiles):
        for l in range(PACK):
            v_scr[PACK * n + l] = tile[:, COLS * l : COLS * (l + 1)]


def near_field(g, idx_ref, copies, near_scr, v_scr):
    cols = []
    for i in range(PACK * g, PACK * (g + 1)):
        copies[i].wait()
        parts = [near_scr[i, :, ROWS * k : ROWS * (k + 1), :].reshape(PANEL, PANEL) for k in range(NEAR_K)]
        rhs = jnp.concatenate([v_scr[idx_ref[i, k]] for k in range(NEAR_K)], axis=0)
        cols.append(dot(jnp.concatenate(parts, axis=1), rhs))
    return jnp.concatenate(cols, axis=1)


def first_kernel(
    far_ref, idx_ref, pc_ref, w_ref, t_ref, recv_ref, lo_ref, hi_ref,
    out_ref, par_ref, bottom_ref, top_ref, cpl_ref, u_ref,
    near_scr, own_scr, c_scr, rhs_scr, v_scr, sems, own_sem,
):
    own = pltpu.make_async_copy(w_ref.at[:, pl.ds(BAS0, HELD - BAS0), :], own_scr, own_sem)
    own.start()
    copies = near_copies(w_ref, near_scr, sems)
    for copy in copies:
        copy.start()
    tiles = [lo_ref[...]] + [recv_ref[:, ROWS * g : ROWS * (g + 1), :] for g in range(GROUPS)] + [hi_ref[...]]
    unpack([tile.reshape(PANEL, 128) for tile in tiles], v_scr)
    own.wait()
    for y in range(SHARES):
        rows = own_scr[y, CPL0 - BAS0 :, :].astype(F32).reshape(FAR_K, 8, 128)
        c_scr[:, 8 * y : 8 * y + 8, :] = rows
    cpl = [c_scr[:, 32 * h : 32 * (h + 1), :].reshape(HALF, 128).T.astype(BF) for h in range(2)]
    for h in range(2):
        cpl_ref[h] = cpl[h]
    zero = jnp.zeros((RANK, RANK), BF)
    for m in range(LEAVES // 2):
        rows = own_scr[:, ROWS * m : ROWS * (m + 1), :].reshape(PANEL, 128)
        upper = jnp.concatenate([t_ref[2 * m], zero], axis=1)
        lower = jnp.concatenate([zero, t_ref[2 * m + 1]], axis=1)
        pair = dot(rows, jnp.concatenate([upper, lower], axis=0)).astype(BF)
        u_ref[m // 2, :, 128 * (m % 2) : 128 * (m % 2 + 1)] = pair
    coef = far_sums(far_ref, pc_ref, cpl, rhs_scr)
    group = lane_group((RANK, 128))
    parents = [jnp.zeros((RANK, 128), F32), jnp.zeros((RANK, 128), F32)]
    for g in range(GROUPS):
        u = u_ref[g]
        res = (near_field(g, idx_ref, copies, near_scr, v_scr) + far_field(u, coef[g // 2])).astype(BF)
        tile = res.reshape(SHARES, ROWS, 128)
        out_ref[:, g] = tile
        if g == 0:
            bottom_ref[...] = tile
        if g == GROUPS - 1:
            top_ref[...] = tile
        x = dot_top(u, res)
        for l in range(PACK):
            parents[g // 2] += jnp.where(group == l, x[RANK * l : RANK * (l + 1)], 0.0)
    packed = pack_parents(spread(parents[0]), spread(parents[1]))
    par_ref[...] = jnp.broadcast_to(packed[None], par_ref.shape)


def near_kernel(idx_ref, w_ref, vec_ref, lo_ref, hi_ref, out_ref, near_scr, v_scr, sems):
    copies = near_copies(w_ref, near_scr, sems)
    for copy in copies:
        copy.start()
    tiles = [lo_ref[...]] + [vec_ref[:, g] for g in range(GROUPS)] + [hi_ref[...]]
    unpack([tile.reshape(PANEL, 128) for tile in tiles], v_scr)
    for g in range(GROUPS):
        out_ref[g] = near_field(g, idx_ref, copies, near_scr, v_scr)


def last_kernel(far_ref, pc_ref, cpl_ref, u_ref, near_ref, own_ref, out_ref, rhs_scr):
    coef = far_sums(far_ref, pc_ref, (cpl_ref[0], cpl_ref[1]), rhs_scr)
    for g in range(GROUPS):
        res = (near_ref[g] + far_field(u_ref[g], coef[g // 2])).astype(BF)
        out_ref[:, 0, g] = own_ref[:, g]
        out_ref[:, 1, g] = res.reshape(SHARES, ROWS, 128)


def finish_kernel(recv_ref, first_ref, second_ref):
    for o, ref in enumerate((first_ref, second_ref)):
        for g in range(GROUPS):
            for b in range(2):
                tiles = [recv_ref[PACK * b + s, o, g] for s in range(PACK)]
                for l in range(PACK):
                    cut = slice(COLS * l, COLS * (l + 1))
                    ref[PACK * g + l, :, 128 * b : 128 * (b + 1)] = jnp.concatenate([t[:, cut] for t in tiles], axis=1)


def array(*shape, dtype=BF):
    return jax.ShapeDtypeStruct(shape, dtype)


def call(kernel, name, outs, ins, scratch, flops, nbytes, *operands):
    single = not isinstance(outs, tuple)
    return pl.pallas_call(
        kernel,
        out_shape=outs,
        in_specs=ins,
        out_specs=VMEM if single else (VMEM,) * len(outs),
        scratch_shapes=scratch,
        cost_estimate=pl.CostEstimate(flops=flops, bytes_accessed=nbytes, transcendentals=0),
        name=name,
    )(*operands)


def gather_parents(packed):
    plane = lax.all_to_all(packed, ("x", "z"), 0, 0)
    return lax.all_gather(plane, "core", axis=0)


def halo(bottom, top):
    count = 64
    forward = [(i, i + 1) for i in range(count - 1)]
    backward = [(target, source) for source, target in forward]
    return lax.ppermute(top, CLUS, forward), lax.ppermute(bottom, CLUS, backward)


def body(density, near_list, far_list, near_blocks, basis, transfer, coupling):
    share = array(SHARES, ROWS, 128)
    spread_out = array(PLANE, 32, 128)
    near_scratch = pltpu.VMEM((LEAVES, SHARES, NEAR_K * ROWS, PANEL), BF)
    vec_scratch = pltpu.VMEM((LEAVES + 2 * NWIN, PANEL, COLS), BF)
    rhs_scratch = pltpu.VMEM((HALF, 128), BF)
    near_sems = pltpu.SemaphoreType.DMA((LEAVES,))

    mine = call(
        stack_kernel, "stack", array(HELD, PANEL), [VMEM] * 3, [], 0, 1_400_000,
        near_blocks, basis, jnp.swapaxes(coupling, 2, 3),
    )
    held = lax.all_gather(mine, "y", axis=0)
    near_idx = near_list - (lax.axis_index(CLUS) * LEAVES - NWIN)
    near_idx = jnp.clip(near_idx, 0, LEAVES + 2 * NWIN - 1)
    sent = call(
        prepare_kernel, "prepare", array(SHARES, SENT, 128), [VMEM] * 3, [], 40_000_000, 500_000,
        density, basis, transfer,
    )
    recv = lax.all_to_all(sent, "y", 0, 0)
    parents, bottom, top = call(
        parent_kernel, "parents", (spread_out, share, share), [VMEM], [], 100_000, 500_000, recv
    )
    every = gather_parents(parents)
    low, high = halo(bottom, top)
    first, parents, bottom, top, cpl, u = call(
        first_kernel, "first",
        (
            array(SHARES, GROUPS, ROWS, 128), spread_out, share, share,
            array(2, 2 * RANK, HALF), array(GROUPS, PANEL, PACK * RANK),
        ),
        [SMEM, SMEM, VMEM, ANY] + [VMEM] * 4,
        [
            near_scratch,
            pltpu.VMEM((SHARES, HELD - BAS0, 128), BF),
            pltpu.VMEM((FAR_K, RANK, 128), F32),
            rhs_scratch,
            vec_scratch,
            near_sems,
            pltpu.SemaphoreType.DMA,
        ],
        400_000_000, 8_000_000,
        far_list, near_idx, every, held, transfer, recv, low, high,
    )
    plane = lax.all_to_all(parents, ("x", "z"), 0, 0)
    low, high = halo(bottom, top)
    near = call(
        near_kernel, "near", array(GROUPS, PANEL, 128, dtype=F32), [SMEM, ANY] + [VMEM] * 3,
        [near_scratch, vec_scratch, near_sems], 300_000_000, 6_000_000,
        near_idx, held, first, low, high,
    )
    every = lax.all_gather(plane, "core", axis=0)
    sent = call(
        last_kernel, "last", array(SHARES, 2, GROUPS, ROWS, 128), [SMEM] + [VMEM] * 5,
        [rhs_scratch], 100_000_000, 2_000_000,
        far_list, every, cpl, u, near, first,
    )
    out = array(LEAVES, ROWS, 256)
    return call(
        finish_kernel, "finish", (out, out), [VMEM], [], 0, 600_000, lax.all_to_all(sent, "y", 0, 0)
    )


def solution(mesh):
    fine = Mesh(mesh.devices.reshape(4, 8, 2, 8), ("x", "z", "core", "y"))
    placed = (
        P(CLUS, "y", None),
        P(CLUS, None),
        P(CLUS, None),
        P(CLUS, None, "y", None),
        P(CLUS, "y", None),
        P(CLUS, None, None),
        P(CLUS, None, None, "y"),
    )
    return jax.shard_map(
        body,
        mesh=fine,
        in_specs=placed,
        out_specs=(P(CLUS, "y", None), P(CLUS, "y", None)),
        check_vma=False,
    )
```

```python
import jax
import jax.numpy as jnp
from jax import lax
from jax.experimental import pallas as pl
from jax.experimental.pallas import tpu as pltpu
from jax.sharding import Mesh
from jax.sharding import PartitionSpec as P

BF = jnp.bfloat16
F32 = jnp.float32
LEAVES = 16
ROWS = 16
PANEL = 128
RANK = 64
VECS = 256
COLS = 32
PACK = 4
GROUPS = LEAVES // PACK
NEAR_K = 9
FAR_K = 27
NWIN = 4
WIDE = LEAVES + 2 * NWIN
BAND = 2 * NWIN + 1
SHARES = 8
PLANE = 32
PAIRS = 14
CPL = PAIRS * 8 // ROWS
FULL = WIDE + CPL
HALF = FAR_K * 32
CLUS = ("x", "z", "core")
TOP = (((0,), (0,)), ((), ()))
ANY = pl.BlockSpec(memory_space=pl.ANY)
SMEM = pl.BlockSpec(memory_space=pltpu.SMEM)
VMEM = pl.BlockSpec(memory_space=pltpu.VMEM)


def dot(a, b):
    return jnp.dot(a, b, preferred_element_type=F32)


def dot_top(a, b):
    return lax.dot_general(a, b, TOP, preferred_element_type=F32)


def lane_group(shape):
    return lax.broadcasted_iota(jnp.int32, shape, len(shape) - 1) // COLS


def spread(rows):
    rows = rows + pltpu.roll(rows, 64, 1)
    return rows + pltpu.roll(rows, 32, 1)


def pack_parents(first, second):
    group = lane_group((32, 128))
    low = jnp.where(group == 0, first[:32], first[32:])
    high = jnp.where(group == 2, second[:32], second[32:])
    return jnp.where(group < 2, low, high)


def cut_parents(part, s):
    cut = slice(COLS * s, COLS * (s + 1))
    pieces = [part[0][:32, cut], part[0][32:, cut], part[1][:32, cut], part[1][32:, cut]]
    return jnp.concatenate(pieces, axis=1).astype(BF)


def prepare_kernel(d_ref, b_ref, t_ref, sent_ref, u_ref, ug_ref):
    u = [dot(b_ref[i], t_ref[i]).astype(BF) for i in range(LEAVES)]
    for g in range(GROUPS):
        ug_ref[g] = jnp.concatenate(u[PACK * g : PACK * (g + 1)], axis=1)
    part = []
    for p in range(2):
        rows = jnp.concatenate(u[8 * p : 8 * p + 8], axis=0)
        u_ref[p] = rows
        part.append(dot_top(rows, d_ref[8 * p : 8 * p + 8].reshape(8 * ROWS, VECS)))
    for s in range(SHARES):
        sent_ref[s] = cut_parents(part, s)


def stack_kernel(d_ref, lo_ref, hi_ref, c_ref, out_ref):
    out_ref[:NWIN] = lo_ref[...]
    out_ref[NWIN : NWIN + LEAVES] = d_ref[...]
    out_ref[NWIN + LEAVES : WIDE] = hi_ref[...]
    both = jnp.concatenate([c_ref[0].astype(F32), c_ref[1].astype(F32)], axis=2)
    rest = jnp.concatenate([both[PAIRS:], jnp.zeros((2 * PAIRS - FAR_K, 8, 128), F32)], axis=0)
    both = jnp.concatenate([both[:PAIRS], rest], axis=2)
    out_ref[WIDE:] = both.reshape(CPL, ROWS, VECS).astype(BF)


def parent_kernel(recv_ref, out_ref):
    total = jnp.sum(recv_ref[...].astype(F32), axis=0).astype(BF)
    out_ref[...] = jnp.broadcast_to(total[None], out_ref.shape)


def build_band(idx_ref, near_ref, s_scr):
    s_scr[...] = jnp.zeros_like(s_scr)
    for i in range(LEAVES):
        blocks = [near_ref[i, k].astype(F32) for k in range(NEAR_K)]
        for j in range(i, i + BAND):
            total = jnp.zeros((ROWS, PANEL), F32)
            for k in range(NEAR_K):
                total = total + jnp.where(idx_ref[i, k] == j, blocks[k], 0.0)
            s_scr[j, ROWS * i : ROWS * (i + 1)] = total.astype(BF)
    return jnp.concatenate([s_scr[j] for j in range(WIDE)], axis=1)


def near_kernel(
    idx_ref, near_ref, held_ref, u_ref, ug_ref, order_ref,
    keep_ref, wide_ref, lo_ref, hi_ref, sent_ref,
    s_scr, w_scr, sem,
):
    del order_ref
    copy = pltpu.make_async_copy(held_ref.at[:, pl.ds(0, WIDE)], w_scr, sem)
    copy.start()
    band = build_band(idx_ref, near_ref, s_scr)
    copy.wait()
    res = dot(band, jnp.concatenate([w_scr[:, j].reshape(PANEL, VECS) for j in range(WIDE)], axis=0))
    keep_ref[...] = res.reshape(LEAVES, ROWS, VECS)
    low = res.astype(BF)
    wide = low.reshape(LEAVES, ROWS, VECS)
    wide_ref[:LEAVES] = wide
    wide_ref[LEAVES:] = ug_ref[...]
    lo_ref[:NWIN] = wide[:NWIN]
    lo_ref[NWIN] = ug_ref[0]
    hi_ref[:NWIN] = wide[LEAVES - NWIN :]
    hi_ref[NWIN] = ug_ref[GROUPS - 1]
    part = [dot_top(u_ref[p], low[PANEL * p : PANEL * (p + 1)]) for p in range(2)]
    gram = jnp.concatenate([dot_top(u_ref[p], u_ref[p]) for p in range(2)], axis=1).astype(BF)
    for s in range(SHARES):
        sent_ref[s, :32] = cut_parents(part, s)
        sent_ref[s, 32:] = gram


def widen_kernel(own_ref, lo_ref, hi_ref, out_ref):
    out_ref[:NWIN] = lo_ref[:NWIN]
    out_ref[NWIN : NWIN + LEAVES] = own_ref[:LEAVES]
    out_ref[NWIN + LEAVES : WIDE] = hi_ref[:NWIN]
    out_ref[WIDE] = lo_ref[NWIN]
    out_ref[WIDE + 1 : WIDE + 1 + GROUPS] = own_ref[LEAVES:]
    out_ref[WIDE + 1 + GROUPS] = hi_ref[NWIN]


def second_kernel(idx_ref, near_ref, wide_ref, out_ref, q_ref, s_scr, w_scr, sem):
    copy = pltpu.make_async_copy(wide_ref, w_scr, sem)
    copy.start()
    band = build_band(idx_ref, near_ref, s_scr)
    copy.wait()
    out_ref[...] = dot(band, jnp.concatenate([w_scr[:, j].reshape(PANEL, VECS) for j in range(WIDE)], axis=0))
    parts = []
    for groups in ((0,), (1, 2), (3, 4), (5,)):
        rows = []
        for g in groups:
            u = w_scr[:, WIDE + g].reshape(PANEL, PACK * RANK)
            rows += [u[:, RANK * l : RANK * (l + 1)] for l in range(PACK)]
        cut = band[:, PANEL * PACK * groups[0] : PANEL * PACK * (groups[-1] + 1)]
        parts.append(dot(cut, jnp.concatenate(rows, axis=0)))
    q_ref[...] = jnp.concatenate(parts, axis=1).astype(BF)


def far_sums(far_ref, pc_ref, cpl, rhs_scr):
    side = lax.broadcasted_iota(jnp.int32, (32, 128), 1) // 64
    even = lane_group((RANK, 128)) % 2 == 0
    sums = []
    for p in range(2):
        for k in range(FAR_K):
            parent = far_ref[p, k]
            tile = pc_ref[(parent // 2) % 2, parent // 4]
            rhs_scr[32 * k : 32 * (k + 1), :] = jnp.where(side == parent % 2, tile, jnp.zeros_like(tile))
        rhs = rhs_scr[...]
        acc0 = dot(cpl[0][RANK * p : RANK * (p + 1)], rhs)
        acc1 = dot(cpl[1][RANK * p : RANK * (p + 1)], rhs)
        sums.append(spread(jnp.where(even, acc0, acc1)).astype(BF))
    return sums


def coupling_kernel(held_ref, cpl_ref, w_scr, c_scr, sem):
    copy = pltpu.make_async_copy(held_ref.at[:, pl.ds(WIDE, CPL)], w_scr, sem)
    copy.start()
    copy.wait()
    for y in range(SHARES):
        rows = w_scr[y].astype(F32).reshape(PAIRS, 8, VECS)
        c_scr[:PAIRS, 8 * y : 8 * y + 8, :] = rows[:, :, :128]
        c_scr[PAIRS:, 8 * y : 8 * y + 8, :] = rows[:, :, 128:]
    for h in range(2):
        part = c_scr[:FAR_K, 32 * h : 32 * (h + 1), :]
        cpl_ref[h] = part.reshape(HALF, 128).T.astype(BF)


def middle_kernel(far_ref, pc_ref, cpl_ref, recv_ref, out_ref, tile_ref, rhs_scr):
    coef = far_sums(far_ref, pc_ref, (cpl_ref[0], cpl_ref[1]), rhs_scr)
    tile_ref[...] = pack_parents(coef[0].astype(F32), coef[1].astype(F32)).astype(BF)
    total = jnp.sum(recv_ref[...].astype(F32), axis=0)
    gram = total[32:].astype(BF)
    own = [dot(gram[:, RANK * p : RANK * (p + 1)], coef[p]) for p in range(2)]
    packed = (total[:32] + pack_parents(own[0], own[1])).astype(BF)
    out_ref[...] = jnp.broadcast_to(packed[None], out_ref.shape)


def last_kernel(far_ref, pc_ref, cpl_ref, tile_ref, lo_ref, hi_ref, out_ref, rhs_scr):
    coef = far_sums(far_ref, pc_ref, (cpl_ref[0], cpl_ref[1]), rhs_scr)
    tile = pack_parents(coef[0].astype(F32), coef[1].astype(F32)).astype(BF)
    both = jnp.concatenate([lo_ref[...], tile_ref[...], hi_ref[...], tile], axis=0)
    out_ref[...] = jnp.broadcast_to(both[None], out_ref.shape)


def coefficients(c_ref, kind, p):
    halves = []
    for h in range(2):
        cut = slice(COLS * (2 * p + h), COLS * (2 * p + h + 1))
        pieces = [c_ref[s, 32 * kind : 32 * (kind + 1), cut] for s in range(SHARES)]
        halves.append(jnp.concatenate(pieces, axis=1))
    return jnp.concatenate(halves, axis=0)


def finish_kernel(keep_ref, u_ref, c_ref, near_ref, q_ref, first_ref, second_ref):
    below, above = coefficients(c_ref, 0, 1), coefficients(c_ref, 2, 0)
    own = [coefficients(c_ref, 1, p) for p in range(2)]
    new = [coefficients(c_ref, 3, p) for p in range(2)]
    res = near_ref[...] + dot(q_ref[...], jnp.concatenate([below] + own + [above], axis=0))
    for p in range(2):
        rows = slice(8 * p, 8 * (p + 1))
        far = dot(u_ref[p], own[p]).reshape(8, ROWS, VECS)
        first_ref[rows] = (keep_ref[rows] + far).astype(BF)
        far = dot(u_ref[p], new[p])
        second_ref[rows] = (res[PANEL * p : PANEL * (p + 1)] + far).reshape(8, ROWS, VECS).astype(BF)


def array(*shape, dtype=BF):
    return jax.ShapeDtypeStruct(shape, dtype)


def call(kernel, outs, ins, scratch, flops, nbytes, *operands):
    single = not isinstance(outs, tuple)
    return pl.pallas_call(
        kernel,
        out_shape=outs,
        in_specs=ins,
        out_specs=VMEM if single else (VMEM,) * len(outs),
        scratch_shapes=scratch,
        cost_estimate=pl.CostEstimate(flops=flops, bytes_accessed=nbytes, transcendentals=0),
    )(*operands)


def halo(bottom, top):
    count = 64
    forward = [(i, i + 1) for i in range(count - 1)]
    backward = [(target, source) for source, target in forward]
    return lax.ppermute(top, CLUS, forward), lax.ppermute(bottom, CLUS, backward)


def operator_twice(density, near_list, far_list, near_blocks, basis, transfer, coupling):
    rhs_scratch = pltpu.VMEM((HALF, 128), BF)
    tile = array(32, 128)
    plane_out = array(PLANE, 32, 128)
    cpl_out = array(2, 2 * RANK, HALF)

    low, high = halo(density[:NWIN], density[LEAVES - NWIN :])
    mine = call(
        stack_kernel, array(FULL, ROWS, VECS), [VMEM] * 4, [], 0, 600_000,
        density, low, high, jnp.swapaxes(coupling, 2, 3),
    )
    held = lax.all_gather(mine, "y", axis=0)
    sent, u, ug = call(
        prepare_kernel,
        (array(SHARES, 32, 128), array(2, PANEL, RANK), array(GROUPS, ROWS, PACK * RANK)),
        [VMEM] * 3, [], 40_000_000, 500_000,
        density, basis, transfer,
    )
    recv = lax.all_to_all(sent, "y", 0, 0)
    parents = call(parent_kernel, plane_out, [VMEM], [], 100_000, 300_000, recv)
    plane = lax.all_to_all(parents, ("x", "z"), 0, 0)

    near_idx = near_list - (lax.axis_index(CLUS) * LEAVES - NWIN)
    near_idx = jnp.clip(near_idx, 0, WIDE - 1)
    band_scratch = pltpu.VMEM((WIDE, LEAVES * ROWS, PANEL), BF)
    keep, wide, bottom, top, sent = call(
        near_kernel,
        (
            array(LEAVES, ROWS, VECS, dtype=F32),
            array(LEAVES + GROUPS, ROWS, VECS),
            array(NWIN + 1, ROWS, VECS),
            array(NWIN + 1, ROWS, VECS),
            array(SHARES, 96, 128),
        ),
        [SMEM, VMEM, ANY, VMEM, VMEM, ANY],
        [band_scratch, pltpu.VMEM((SHARES, WIDE, ROWS, VECS), BF), pltpu.SemaphoreType.DMA],
        420_000_000, 4_500_000,
        near_idx, near_blocks, held, u, ug, parents,
    )
    low, high = halo(bottom, top)
    wide = call(
        widen_kernel, array(WIDE + GROUPS + 2, ROWS, VECS), [VMEM] * 3, [], 0, 500_000,
        wide, low, high,
    )
    wide = lax.all_gather(wide, "y", axis=0)
    recv = lax.all_to_all(sent, "y", 0, 0)

    cpl = call(
        coupling_kernel, cpl_out, [ANY],
        [
            pltpu.VMEM((SHARES, CPL, ROWS, VECS), BF),
            pltpu.VMEM((2 * PAIRS, RANK, 128), F32),
            pltpu.SemaphoreType.DMA,
        ],
        0, 1_000_000, held,
    )
    every = lax.all_gather(plane, "core", axis=0)
    parents, own = call(
        middle_kernel, (plane_out, tile), [SMEM] + [VMEM] * 3, [rhs_scratch], 100_000_000, 1_400_000,
        far_list, every, cpl, recv,
    )
    plane = lax.all_to_all(parents, ("x", "z"), 0, 0)
    low, high = halo(own, own)
    every = lax.all_gather(plane, "core", axis=0)
    sent = call(
        last_kernel, array(SHARES, 128, 128), [SMEM] + [VMEM] * 5, [rhs_scratch], 100_000_000, 1_300_000,
        far_list, every, cpl, own, low, high,
    )
    coefs = lax.all_to_all(sent, "y", 0, 0)
    plain, q = call(
        second_kernel,
        (array(LEAVES * ROWS, VECS, dtype=F32), array(LEAVES * ROWS, 4 * RANK)),
        [SMEM, VMEM, ANY],
        [band_scratch, pltpu.VMEM((SHARES, WIDE + GROUPS + 2, ROWS, VECS), BF), pltpu.SemaphoreType.DMA],
        520_000_000, 4_000_000,
        near_idx, near_blocks, wide,
    )
    out = array(LEAVES, ROWS, VECS)
    return call(
        finish_kernel, (out, out), [VMEM] * 5, [], 100_000_000, 2_000_000,
        keep, u, coefs, plain, q,
    )


def solution(mesh):
    fine = Mesh(mesh.devices.reshape(4, 8, 2, 8), ("x", "z", "core", "y"))
    placed = (
        P(CLUS, "y", None),
        P(CLUS, None),
        P(CLUS, None),
        P(CLUS, None, "y", None),
        P(CLUS, "y", None),
        P(CLUS, None, None),
        P(CLUS, None, None, "y"),
    )
    return jax.shard_map(
        operator_twice,
        mesh=fine,
        in_specs=placed,
        out_specs=(P(CLUS, "y", None), P(CLUS, "y", None)),
        check_vma=False,
    )
```

```python
import jax
import jax.numpy as jnp
from jax import lax
from jax.experimental import pallas as pl
from jax.experimental.pallas import tpu as pltpu
from jax.sharding import Mesh
from jax.sharding import PartitionSpec as P

BF = jnp.bfloat16
F32 = jnp.float32
LEAVES = 16
ROWS = 16
PANEL = 128
RANK = 64
VECS = 256
COLS = 32
PACK = 4
GROUPS = LEAVES // PACK
NEAR_K = 9
FAR_K = 27
NWIN = 4
WIDE = LEAVES + 2 * NWIN
BAND = 2 * NWIN + 1
SHARES = 8
PLANE = 32
PAIRS = 14
CPL = PAIRS * 8 // ROWS
FULL = 16
HALF = FAR_K * 32
CLUS = ("x", "z", "core")
TOP = (((0,), (0,)), ((), ()))
ANY = pl.BlockSpec(memory_space=pl.ANY)
SMEM = pl.BlockSpec(memory_space=pltpu.SMEM)
VMEM = pl.BlockSpec(memory_space=pltpu.VMEM)


def dot(a, b):
    return jnp.dot(a, b, preferred_element_type=F32)


def dot_top(a, b):
    return lax.dot_general(a, b, TOP, preferred_element_type=F32)


def lane_group(shape):
    return lax.broadcasted_iota(jnp.int32, shape, len(shape) - 1) // COLS


def spread(rows):
    rows = rows + pltpu.roll(rows, 64, 1)
    return rows + pltpu.roll(rows, 32, 1)


def pack_parents(first, second):
    group = lane_group((32, 128))
    low = jnp.where(group == 0, first[:32], first[32:])
    high = jnp.where(group == 2, second[:32], second[32:])
    return jnp.where(group < 2, low, high)


def cut_parents(part, s):
    cut = slice(COLS * s, COLS * (s + 1))
    pieces = [part[0][:32, cut], part[0][32:, cut], part[1][:32, cut], part[1][32:, cut]]
    return jnp.concatenate(pieces, axis=1).astype(BF)


def prepare_kernel(d_ref, b_ref, t_ref, c_ref, sent_ref, u_ref, uc_ref):
    u = [dot(b_ref[i], t_ref[i]).astype(BF) for i in range(LEAVES)]
    part = []
    for p in range(2):
        rows = jnp.concatenate(u[8 * p : 8 * p + 8], axis=0)
        u_ref[p] = rows
        part.append(dot_top(rows, d_ref[8 * p : 8 * p + 8].reshape(8 * ROWS, VECS)))
    for s in range(SHARES):
        tile = cut_parents(part, s)
        sent_ref[s, :LEAVES] = d_ref[...]
        sent_ref[s, LEAVES] = jnp.concatenate([tile[:ROWS], tile[ROWS:]], axis=1)
    for g in range(GROUPS):
        uc_ref[g] = jnp.concatenate(u[PACK * g : PACK * (g + 1)], axis=1)
    both = jnp.concatenate([c_ref[0].astype(F32), c_ref[1].astype(F32)], axis=2)
    rest = jnp.concatenate([both[PAIRS:], jnp.zeros((2 * PAIRS - FAR_K, 8, 128), F32)], axis=0)
    both = jnp.concatenate([both[:PAIRS], rest], axis=2).reshape(CPL, ROWS, VECS).astype(BF)
    uc_ref[GROUPS : GROUPS + CPL] = both
    uc_ref[GROUPS + CPL :] = jnp.zeros((FULL - GROUPS - CPL, ROWS, VECS), BF)


def parent_kernel(recv_ref, out_ref, scr, sem):
    move = pltpu.make_async_copy(recv_ref.at[:, LEAVES], scr, sem)
    move.start()
    move.wait()
    total = jnp.sum(scr[...].astype(F32), axis=0).astype(BF)
    total = jnp.concatenate([total[:, :128], total[:, 128:]], axis=0)
    out_ref[...] = jnp.broadcast_to(total[None], out_ref.shape)


def build_band(idx_ref, near_ref, s_scr):
    offset = lax.axis_index(CLUS) * LEAVES - NWIN
    s_scr[...] = jnp.zeros_like(s_scr)
    for i in range(LEAVES):
        blocks = [near_ref[i, k].astype(F32) for k in range(NEAR_K)]
        for j in range(i, i + BAND):
            total = jnp.zeros((ROWS, PANEL), F32)
            for k in range(NEAR_K):
                total = total + jnp.where(idx_ref[i, k] == j + offset, blocks[k], 0.0)
            s_scr[j, ROWS * i : ROWS * (i + 1)] = total.astype(BF)
    return jnp.concatenate([s_scr[j] for j in range(WIDE)], axis=1)


def fetch(pairs, sems):
    moves = [pltpu.make_async_copy(src, dst, sems.at[n]) for n, (src, dst) in enumerate(pairs)]
    for move in moves:
        move.start()
    return moves


def leaf_rows(w_scr):
    return jnp.concatenate([w_scr[:, j].reshape(PANEL, VECS) for j in range(WIDE)], axis=0)


def near_kernel(
    idx_ref, near_ref, lo_ref, own_ref, hi_ref, u_ref,
    keep_ref, low_ref, sent_ref,
    s_scr, w_scr, sems,
):
    top = NWIN + LEAVES
    pairs = ((lo_ref, w_scr.at[:, :NWIN]), (own_ref.at[:, :LEAVES], w_scr.at[:, NWIN:top]), (hi_ref, w_scr.at[:, top:]))
    moves = fetch(pairs, sems)
    band = build_band(idx_ref, near_ref, s_scr)
    for move in moves:
        move.wait()
    res = dot(band, leaf_rows(w_scr))
    keep_ref[...] = res.reshape(LEAVES, ROWS, VECS)
    low = res.astype(BF)
    low_ref[...] = low.reshape(LEAVES, ROWS, VECS)
    part = [dot_top(u_ref[p], low[PANEL * p : PANEL * (p + 1)]) for p in range(2)]
    gram = jnp.concatenate([dot_top(u_ref[p], u_ref[p]) for p in range(2)], axis=1).astype(BF)
    for s in range(SHARES):
        sent_ref[s, :32] = cut_parents(part, s)
        sent_ref[s, 32:] = gram


def second_kernel(
    idx_ref, near_ref, lo_ref, own_ref, hi_ref, ulo_ref, uc_ref, uhi_ref,
    out_ref, q_ref, s_scr, w_scr, sems,
):
    top = NWIN + LEAVES
    pairs = (
        (lo_ref, w_scr.at[:, :NWIN]),
        (own_ref, w_scr.at[:, NWIN:top]),
        (hi_ref, w_scr.at[:, top:WIDE]),
        (ulo_ref.at[:SHARES], w_scr.at[:, WIDE]),
        (uc_ref.at[:, :GROUPS], w_scr.at[:, WIDE + 1 : WIDE + 1 + GROUPS]),
        (uhi_ref.at[:SHARES], w_scr.at[:, WIDE + 1 + GROUPS]),
    )
    moves = fetch(pairs, sems)
    band = build_band(idx_ref, near_ref, s_scr)
    for move in moves:
        move.wait()
    out_ref[...] = dot(band, leaf_rows(w_scr))
    parts = []
    for groups in ((0,), (1, 2), (3, 4), (5,)):
        rows = []
        for g in groups:
            u = w_scr[:, WIDE + g].reshape(PANEL, PACK * RANK)
            rows += [u[:, RANK * l : RANK * (l + 1)] for l in range(PACK)]
        cut = band[:, PANEL * PACK * groups[0] : PANEL * PACK * (groups[-1] + 1)]
        parts.append(dot(cut, jnp.concatenate(rows, axis=0)))
    q_ref[...] = jnp.concatenate(parts, axis=1).astype(BF)


def far_sums(far_ref, pc_ref, cpl, rhs_scr):
    side = lax.broadcasted_iota(jnp.int32, (32, 128), 1) // 64
    even = lane_group((RANK, 128)) % 2 == 0
    sums = []
    for p in range(2):
        for k in range(FAR_K):
            parent = far_ref[p, k]
            tile = pc_ref[(parent // 2) % 2, parent // 4]
            rhs_scr[32 * k : 32 * (k + 1), :] = jnp.where(side == parent % 2, tile, jnp.zeros_like(tile))
        rhs = rhs_scr[...]
        acc0 = dot(cpl[0][RANK * p : RANK * (p + 1)], rhs)
        acc1 = dot(cpl[1][RANK * p : RANK * (p + 1)], rhs)
        sums.append(spread(jnp.where(even, acc0, acc1)).astype(BF))
    return sums


def coupling_kernel(held_ref, cpl_ref, w_scr, c_scr, sem):
    copy = pltpu.make_async_copy(held_ref.at[:, pl.ds(GROUPS, CPL)], w_scr, sem)
    copy.start()
    copy.wait()
    for y in range(SHARES):
        rows = w_scr[y].astype(F32).reshape(PAIRS, 8, VECS)
        c_scr[:PAIRS, 8 * y : 8 * y + 8, :] = rows[:, :, :128]
        c_scr[PAIRS:, 8 * y : 8 * y + 8, :] = rows[:, :, 128:]
    for h in range(2):
        part = c_scr[:FAR_K, 32 * h : 32 * (h + 1), :]
        cpl_ref[h] = part.reshape(HALF, 128).T.astype(BF)


def fold(tile):
    return jnp.concatenate([tile[:ROWS], tile[ROWS:]], axis=1)


def unfold(slab):
    return jnp.concatenate([slab[:, :128], slab[:, 128:]], axis=0)


def middle_kernel(
    far_ref, pc_ref, cpl_ref, recv_ref, held_ref, out_ref, bottom_ref, top_ref, rhs_scr, u_scr, sems
):
    pairs = ((held_ref.at[:, 0], u_scr.at[0]), (held_ref.at[:, GROUPS - 1], u_scr.at[1]))
    moves = fetch(pairs, sems)
    coef = far_sums(far_ref, pc_ref, (cpl_ref[0], cpl_ref[1]), rhs_scr)
    slab = fold(pack_parents(coef[0].astype(F32), coef[1].astype(F32)).astype(BF))
    for n, ref in enumerate((bottom_ref, top_ref)):
        moves[n].wait()
        ref[:SHARES] = u_scr[n]
        ref[SHARES] = slab
    total = jnp.sum(recv_ref[...].astype(F32), axis=0)
    gram = total[32:].astype(BF)
    own = [dot(gram[:, RANK * p : RANK * (p + 1)], coef[p]) for p in range(2)]
    packed = (total[:32] + pack_parents(own[0], own[1])).astype(BF)
    out_ref[...] = jnp.broadcast_to(packed[None], out_ref.shape)


def last_kernel(far_ref, pc_ref, cpl_ref, own_ref, lo_ref, hi_ref, out_ref, rhs_scr):
    coef = far_sums(far_ref, pc_ref, (cpl_ref[0], cpl_ref[1]), rhs_scr)
    tile = pack_parents(coef[0].astype(F32), coef[1].astype(F32)).astype(BF)
    both = [unfold(ref[SHARES]) for ref in (lo_ref, own_ref, hi_ref)] + [tile]
    both = jnp.concatenate(both, axis=0)
    out_ref[...] = jnp.broadcast_to(both[None], out_ref.shape)


def coefficients(c_ref, kind, p):
    halves = []
    for h in range(2):
        cut = slice(COLS * (2 * p + h), COLS * (2 * p + h + 1))
        pieces = [c_ref[s, 32 * kind : 32 * (kind + 1), cut] for s in range(SHARES)]
        halves.append(jnp.concatenate(pieces, axis=1))
    return jnp.concatenate(halves, axis=0)


def finish_kernel(keep_ref, u_ref, c_ref, near_ref, q_ref, first_ref, second_ref):
    below, above = coefficients(c_ref, 0, 1), coefficients(c_ref, 2, 0)
    own = [coefficients(c_ref, 1, p) for p in range(2)]
    new = [coefficients(c_ref, 3, p) for p in range(2)]
    res = near_ref[...] + dot(q_ref[...], jnp.concatenate([below] + own + [above], axis=0))
    for p in range(2):
        rows = slice(8 * p, 8 * (p + 1))
        far = dot(u_ref[p], own[p]).reshape(8, ROWS, VECS)
        first_ref[rows] = (keep_ref[rows] + far).astype(BF)
        far = dot(u_ref[p], new[p])
        second_ref[rows] = (res[PANEL * p : PANEL * (p + 1)] + far).reshape(8, ROWS, VECS).astype(BF)


def array(*shape, dtype=BF):
    return jax.ShapeDtypeStruct(shape, dtype)


def call(kernel, outs, ins, scratch, flops, nbytes, *operands):
    single = not isinstance(outs, tuple)
    return pl.pallas_call(
        kernel,
        out_shape=outs,
        in_specs=ins,
        out_specs=VMEM if single else (VMEM,) * len(outs),
        scratch_shapes=scratch,
        cost_estimate=pl.CostEstimate(flops=flops, bytes_accessed=nbytes, transcendentals=0),
    )(*operands)


def halo(bottom, top):
    count = 64
    forward = [(i, i + 1) for i in range(count - 1)]
    backward = [(target, source) for source, target in forward]
    return lax.ppermute(top, CLUS, forward), lax.ppermute(bottom, CLUS, backward)


def exchange(values, axis):
    return lax.all_to_all(values, axis, 0, 0)


def operator_twice(density, near_list, far_list, near_blocks, basis, transfer, coupling):
    rhs_scratch = pltpu.VMEM((HALF, 128), BF)
    band_scratch = pltpu.VMEM((WIDE, LEAVES * ROWS, PANEL), BF)
    plane_out = array(PLANE, 32, 128)
    cpl_out = array(2, 2 * RANK, HALF)
    sent, u, uc = call(
        prepare_kernel,
        (
            array(SHARES, LEAVES + 1, ROWS, VECS),
            array(2, PANEL, RANK),
            array(FULL, ROWS, VECS),
        ),
        [VMEM] * 4, [], 40_000_000, 1_700_000,
        density, basis, transfer, jnp.swapaxes(coupling, 2, 3),
    )
    held = lax.all_gather(uc, "y", axis=0)
    whole = exchange(sent, "y")
    parents = call(
        parent_kernel, plane_out, [ANY],
        [pltpu.VMEM((SHARES, ROWS, VECS), BF), pltpu.SemaphoreType.DMA], 100_000, 300_000,
        whole,
    )
    plane = exchange(parents, ("x", "z"))

    low, high = halo(whole[:, :NWIN], whole[:, LEAVES - NWIN : LEAVES])
    keep, wide, sent = call(
        near_kernel,
        (
            array(LEAVES, ROWS, VECS, dtype=F32),
            array(LEAVES, ROWS, VECS),
            array(SHARES, 96, 128),
        ),
        [SMEM, VMEM, ANY, ANY, ANY, VMEM],
        [band_scratch, pltpu.VMEM((SHARES, WIDE, ROWS, VECS), BF), pltpu.SemaphoreType.DMA((3,))],
        420_000_000, 4_500_000,
        near_list, near_blocks, low, whole, high, u,
    )
    wide = lax.all_gather(wide, "y", axis=0)
    recv = exchange(sent, "y")

    cpl = call(
        coupling_kernel, cpl_out, [ANY],
        [
            pltpu.VMEM((SHARES, CPL, ROWS, VECS), BF),
            pltpu.VMEM((2 * PAIRS, RANK, 128), F32),
            pltpu.SemaphoreType.DMA,
        ],
        0, 1_000_000, held,
    )
    every = lax.all_gather(plane, "core", axis=0)
    payload = array(SHARES + 1, ROWS, VECS)
    parents, bottom, top = call(
        middle_kernel, (plane_out, payload, payload),
        [SMEM] + [VMEM] * 3 + [ANY],
        [rhs_scratch, pltpu.VMEM((2, SHARES, ROWS, VECS), BF), pltpu.SemaphoreType.DMA((2,))],
        100_000_000, 1_700_000,
        far_list, every, cpl, recv, held,
    )
    plane = exchange(parents, ("x", "z"))
    below, above = halo(bottom, top)
    every = lax.all_gather(plane, "core", axis=0)
    sent = call(
        last_kernel, array(SHARES, 128, 128), [SMEM] + [VMEM] * 5, [rhs_scratch], 100_000_000, 1_300_000,
        far_list, every, cpl, bottom, below, above,
    )
    coefs = exchange(sent, "y")
    low, high = halo(wide[:, :NWIN], wide[:, LEAVES - NWIN :])
    plain, q = call(
        second_kernel,
        (array(LEAVES * ROWS, VECS, dtype=F32), array(LEAVES * ROWS, 4 * RANK)),
        [SMEM, VMEM] + [ANY] * 6,
        [
            band_scratch,
            pltpu.VMEM((SHARES, WIDE + GROUPS + 2, ROWS, VECS), BF),
            pltpu.SemaphoreType.DMA((6,)),
        ],
        520_000_000, 4_000_000,
        near_list, near_blocks, low, wide, high, below, held, above,
    )
    out = array(LEAVES, ROWS, VECS)
    return call(
        finish_kernel, (out, out), [VMEM] * 5, [], 100_000_000, 2_000_000,
        keep, u, coefs, plain, q,
    )


def solution(mesh):
    fine = Mesh(mesh.devices.reshape(4, 8, 2, 8), ("x", "z", "core", "y"))
    placed = (
        P(CLUS, "y", None),
        P(CLUS, None),
        P(CLUS, None),
        P(CLUS, None, "y", None),
        P(CLUS, "y", None),
        P(CLUS, None, None),
        P(CLUS, None, None, "y"),
    )
    return jax.shard_map(
        operator_twice,
        mesh=fine,
        in_specs=placed,
        out_specs=(P(CLUS, "y", None), P(CLUS, "y", None)),
        check_vma=False,
    )
```

```python
import jax
import jax.numpy as jnp
from jax import lax
from jax.experimental import pallas as pl
from jax.experimental.pallas import tpu as pltpu
from jax.sharding import Mesh
from jax.sharding import PartitionSpec as P

BF = jnp.bfloat16
F32 = jnp.float32
LEAVES = 16
ROWS = 16
PANEL = 128
RANK = 64
VECS = 256
COLS = 32
PACK = 4
GROUPS = LEAVES // PACK
NEAR_K = 9
FAR_K = 27
NWIN = 4
WIDE = LEAVES + 2 * NWIN
BAND = 2 * NWIN + 1
SHARES = 8
PLANE = 32
PAIRS = 14
CPL = PAIRS * 8 // ROWS
FULL = 16
HALF = FAR_K * 32
CLUS = ("x", "z", "core")
TOP = (((0,), (0,)), ((), ()))
ANY = pl.BlockSpec(memory_space=pl.ANY)
SMEM = pl.BlockSpec(memory_space=pltpu.SMEM)
VMEM = pl.BlockSpec(memory_space=pltpu.VMEM)


def dot(a, b):
    return jnp.dot(a, b, preferred_element_type=F32)


def dot_top(a, b):
    return lax.dot_general(a, b, TOP, preferred_element_type=F32)


def lane_group(shape):
    return lax.broadcasted_iota(jnp.int32, shape, len(shape) - 1) // COLS


def spread(rows):
    rows = rows + pltpu.roll(rows, 64, 1)
    return rows + pltpu.roll(rows, 32, 1)


def pack_parents(first, second):
    group = lane_group((32, 128))
    low = jnp.where(group == 0, first[:32], first[32:])
    high = jnp.where(group == 2, second[:32], second[32:])
    return jnp.where(group < 2, low, high)


def cut_parents(part, s):
    cut = slice(COLS * s, COLS * (s + 1))
    pieces = [part[0][:32, cut], part[0][32:, cut], part[1][:32, cut], part[1][32:, cut]]
    return jnp.concatenate(pieces, axis=1).astype(BF)


def prepare_kernel(d_ref, b_ref, t_ref, c_ref, sent_ref, u_ref, uc_ref):
    u = [dot(b_ref[i], t_ref[i]).astype(BF) for i in range(LEAVES)]
    part = []
    for p in range(2):
        rows = jnp.concatenate(u[8 * p : 8 * p + 8], axis=0)
        u_ref[p] = rows
        part.append(dot_top(rows, d_ref[8 * p : 8 * p + 8].reshape(8 * ROWS, VECS)))
    for s in range(SHARES):
        tile = cut_parents(part, s)
        sent_ref[s, :LEAVES] = d_ref[...]
        sent_ref[s, LEAVES] = jnp.concatenate([tile[:ROWS], tile[ROWS:]], axis=1)
    for g in range(GROUPS):
        uc_ref[g] = jnp.concatenate(u[PACK * g : PACK * (g + 1)], axis=1)
    both = jnp.concatenate([c_ref[0].astype(F32), c_ref[1].astype(F32)], axis=2)
    rest = jnp.concatenate([both[PAIRS:], jnp.zeros((2 * PAIRS - FAR_K, 8, 128), F32)], axis=0)
    both = jnp.concatenate([both[:PAIRS], rest], axis=2).reshape(CPL, ROWS, VECS).astype(BF)
    uc_ref[GROUPS : GROUPS + CPL] = both
    uc_ref[GROUPS + CPL :] = jnp.zeros((FULL - GROUPS - CPL, ROWS, VECS), BF)


def parent_kernel(recv_ref, out_ref, scr, sem):
    move = pltpu.make_async_copy(recv_ref.at[:, LEAVES], scr, sem)
    move.start()
    move.wait()
    total = jnp.sum(scr[...].astype(F32), axis=0).astype(BF)
    total = jnp.concatenate([total[:, :128], total[:, 128:]], axis=0)
    out_ref[...] = jnp.broadcast_to(total[None], out_ref.shape)


def build_band(idx_ref, near_ref, s_scr):
    offset = lax.axis_index(CLUS) * LEAVES - NWIN
    s_scr[...] = jnp.zeros_like(s_scr)
    for i in range(LEAVES):
        blocks = [near_ref[i, k].astype(F32) for k in range(NEAR_K)]
        for j in range(i, i + BAND):
            total = jnp.zeros((ROWS, PANEL), F32)
            for k in range(NEAR_K):
                total = total + jnp.where(idx_ref[i, k] == j + offset, blocks[k], 0.0)
            s_scr[j, ROWS * i : ROWS * (i + 1)] = total.astype(BF)
    return jnp.concatenate([s_scr[j] for j in range(WIDE)], axis=1)


def fetch(pairs, sems):
    moves = [pltpu.make_async_copy(src, dst, sems.at[n]) for n, (src, dst) in enumerate(pairs)]
    for move in moves:
        move.start()
    return moves


def leaf_rows(w_scr):
    return jnp.concatenate([w_scr[:, j].reshape(PANEL, VECS) for j in range(WIDE)], axis=0)


def near_kernel(
    idx_ref, near_ref, lo_ref, own_ref, hi_ref, u_ref,
    keep_ref, low_ref, bottom_ref, top_ref, sent_ref,
    s_scr, w_scr, sems,
):
    top = NWIN + LEAVES
    pairs = ((lo_ref, w_scr.at[:, :NWIN]), (own_ref.at[:, :LEAVES], w_scr.at[:, NWIN:top]), (hi_ref, w_scr.at[:, top:]))
    moves = fetch(pairs, sems)
    band = build_band(idx_ref, near_ref, s_scr)
    for move in moves:
        move.wait()
    res = dot(band, leaf_rows(w_scr))
    keep_ref[...] = res.reshape(LEAVES, ROWS, VECS)
    low = res.astype(BF)
    rows = low.reshape(LEAVES, ROWS, VECS)
    low_ref[...] = rows
    bottom_ref[...] = rows[:NWIN]
    top_ref[...] = rows[LEAVES - NWIN :]
    part = [dot_top(u_ref[p], low[PANEL * p : PANEL * (p + 1)]) for p in range(2)]
    gram = jnp.concatenate([dot_top(u_ref[p], u_ref[p]) for p in range(2)], axis=1).astype(BF)
    for s in range(SHARES):
        sent_ref[s, :32] = cut_parents(part, s)
        sent_ref[s, 32:] = gram


def widen_kernel(lo_ref, own_ref, hi_ref, out_ref):
    out_ref[:NWIN] = lo_ref[...]
    out_ref[NWIN : NWIN + LEAVES] = own_ref[...]
    out_ref[NWIN + LEAVES :] = hi_ref[...]


def second_kernel(
    idx_ref, near_ref, own_ref, ulo_ref, uc_ref, uhi_ref,
    out_ref, q_ref, s_scr, w_scr, sems,
):
    pairs = (
        (own_ref, w_scr.at[:, :WIDE]),
        (ulo_ref.at[:SHARES], w_scr.at[:, WIDE]),
        (uc_ref.at[:, :GROUPS], w_scr.at[:, WIDE + 1 : WIDE + 1 + GROUPS]),
        (uhi_ref.at[:SHARES], w_scr.at[:, WIDE + 1 + GROUPS]),
    )
    moves = fetch(pairs, sems)
    band = build_band(idx_ref, near_ref, s_scr)
    for move in moves:
        move.wait()
    out_ref[...] = dot(band, leaf_rows(w_scr))
    parts = []
    for groups in ((0,), (1, 2), (3, 4), (5,)):
        rows = []
        for g in groups:
            u = w_scr[:, WIDE + g].reshape(PANEL, PACK * RANK)
            rows += [u[:, RANK * l : RANK * (l + 1)] for l in range(PACK)]
        cut = band[:, PANEL * PACK * groups[0] : PANEL * PACK * (groups[-1] + 1)]
        parts.append(dot(cut, jnp.concatenate(rows, axis=0)))
    q_ref[...] = jnp.concatenate(parts, axis=1).astype(BF)


def far_sums(far_ref, pc_ref, cpl, rhs_scr):
    side = lax.broadcasted_iota(jnp.int32, (32, 128), 1) // 64
    even = lane_group((RANK, 128)) % 2 == 0
    sums = []
    for p in range(2):
        for k in range(FAR_K):
            parent = far_ref[p, k]
            tile = pc_ref[(parent // 2) % 2, parent // 4]
            rhs_scr[32 * k : 32 * (k + 1), :] = jnp.where(side == parent % 2, tile, jnp.zeros_like(tile))
        rhs = rhs_scr[...]
        acc0 = dot(cpl[0][RANK * p : RANK * (p + 1)], rhs)
        acc1 = dot(cpl[1][RANK * p : RANK * (p + 1)], rhs)
        sums.append(spread(jnp.where(even, acc0, acc1)).astype(BF))
    return sums


def coupling_kernel(held_ref, cpl_ref, w_scr, c_scr, sem):
    copy = pltpu.make_async_copy(held_ref.at[:, pl.ds(GROUPS, CPL)], w_scr, sem)
    copy.start()
    copy.wait()
    for y in range(SHARES):
        rows = w_scr[y].astype(F32).reshape(PAIRS, 8, VECS)
        c_scr[:PAIRS, 8 * y : 8 * y + 8, :] = rows[:, :, :128]
        c_scr[PAIRS:, 8 * y : 8 * y + 8, :] = rows[:, :, 128:]
    for h in range(2):
        part = c_scr[:FAR_K, 32 * h : 32 * (h + 1), :]
        cpl_ref[h] = part.reshape(HALF, 128).T.astype(BF)


def fold(tile):
    return jnp.concatenate([tile[:ROWS], tile[ROWS:]], axis=1)


def unfold(slab):
    return jnp.concatenate([slab[:, :128], slab[:, 128:]], axis=0)


def middle_kernel(
    far_ref, pc_ref, cpl_ref, recv_ref, held_ref, out_ref, bottom_ref, top_ref,
    rhs_scr, u_scr, recv_scr, sems,
):
    pairs = (
        (held_ref.at[:, 0], u_scr.at[0]),
        (held_ref.at[:, GROUPS - 1], u_scr.at[1]),
        (recv_ref, recv_scr),
    )
    moves = fetch(pairs, sems)
    coef = far_sums(far_ref, pc_ref, (cpl_ref[0], cpl_ref[1]), rhs_scr)
    slab = fold(pack_parents(coef[0].astype(F32), coef[1].astype(F32)).astype(BF))
    for n, ref in enumerate((bottom_ref, top_ref)):
        moves[n].wait()
        ref[:SHARES] = u_scr[n]
        ref[SHARES] = slab
    moves[2].wait()
    total = jnp.sum(recv_scr[...].astype(F32), axis=0)
    gram = total[32:].astype(BF)
    own = [dot(gram[:, RANK * p : RANK * (p + 1)], coef[p]) for p in range(2)]
    packed = (total[:32] + pack_parents(own[0], own[1])).astype(BF)
    out_ref[...] = jnp.broadcast_to(packed[None], out_ref.shape)


def last_kernel(far_ref, pc_ref, cpl_ref, own_ref, lo_ref, hi_ref, out_ref, rhs_scr, t_scr, sems):
    pairs = [(ref.at[SHARES], t_scr.at[n]) for n, ref in enumerate((lo_ref, own_ref, hi_ref))]
    moves = fetch(pairs, sems)
    coef = far_sums(far_ref, pc_ref, (cpl_ref[0], cpl_ref[1]), rhs_scr)
    tile = pack_parents(coef[0].astype(F32), coef[1].astype(F32)).astype(BF)
    for move in moves:
        move.wait()
    both = [unfold(t_scr[n]) for n in range(3)] + [tile]
    both = jnp.concatenate(both, axis=0)
    out_ref[...] = jnp.broadcast_to(both[None], out_ref.shape)


def coefficients(c_ref, kind, p):
    halves = []
    for h in range(2):
        cut = slice(COLS * (2 * p + h), COLS * (2 * p + h + 1))
        pieces = [c_ref[s, 32 * kind : 32 * (kind + 1), cut] for s in range(SHARES)]
        halves.append(jnp.concatenate(pieces, axis=1))
    return jnp.concatenate(halves, axis=0)


def finish_kernel(
    keep_ref, u_ref, recv_ref, near_ref, q_ref, first_ref, second_ref, c_ref, sems
):
    for move in fetch(((recv_ref, c_ref),), sems):
        move.wait()
    below, above = coefficients(c_ref, 0, 1), coefficients(c_ref, 2, 0)
    own = [coefficients(c_ref, 1, p) for p in range(2)]
    new = [coefficients(c_ref, 3, p) for p in range(2)]
    res = near_ref[...] + dot(q_ref[...], jnp.concatenate([below] + own + [above], axis=0))
    for p in range(2):
        rows = slice(8 * p, 8 * (p + 1))
        far = dot(u_ref[p], own[p]).reshape(8, ROWS, VECS)
        first_ref[rows] = (keep_ref[rows] + far).astype(BF)
        far = dot(u_ref[p], new[p])
        second_ref[rows] = (res[PANEL * p : PANEL * (p + 1)] + far).reshape(8, ROWS, VECS).astype(BF)


def array(*shape, dtype=BF):
    return jax.ShapeDtypeStruct(shape, dtype)


def call(kernel, outs, ins, scratch, flops, nbytes, *operands):
    single = not isinstance(outs, tuple)
    return pl.pallas_call(
        kernel,
        out_shape=outs,
        in_specs=ins,
        out_specs=VMEM if single else (VMEM,) * len(outs),
        scratch_shapes=scratch,
        cost_estimate=pl.CostEstimate(flops=flops, bytes_accessed=nbytes, transcendentals=0),
    )(*operands)


def halo(bottom, top):
    count = 64
    forward = [(i, i + 1) for i in range(count - 1)]
    backward = [(target, source) for source, target in forward]
    return lax.ppermute(top, CLUS, forward), lax.ppermute(bottom, CLUS, backward)


def exchange(values, axis):
    return lax.all_to_all(values, axis, 0, 0)


def operator_twice(density, near_list, far_list, near_blocks, basis, transfer, coupling):
    rhs_scratch = pltpu.VMEM((HALF, 128), BF)
    band_scratch = pltpu.VMEM((WIDE, LEAVES * ROWS, PANEL), BF)
    plane_out = array(PLANE, 32, 128)
    cpl_out = array(2, 2 * RANK, HALF)
    sent, u, uc = call(
        prepare_kernel,
        (
            array(SHARES, LEAVES + 1, ROWS, VECS),
            array(2, PANEL, RANK),
            array(FULL, ROWS, VECS),
        ),
        [VMEM] * 4, [], 40_000_000, 1_700_000,
        density, basis, transfer, jnp.swapaxes(coupling, 2, 3),
    )
    whole = exchange(sent, "y")
    uc, whole = lax.optimization_barrier((uc, whole))
    held = lax.all_gather(uc, "y", axis=0)
    parents = call(
        parent_kernel, plane_out, [ANY],
        [pltpu.VMEM((SHARES, ROWS, VECS), BF), pltpu.SemaphoreType.DMA], 100_000, 300_000,
        whole,
    )
    plane = exchange(parents, ("x", "z"))

    low, high = halo(whole[:, :NWIN], whole[:, LEAVES - NWIN : LEAVES])
    keep, wide, bottom, top, sent = call(
        near_kernel,
        (
            array(LEAVES, ROWS, VECS, dtype=F32),
            array(LEAVES, ROWS, VECS),
            array(NWIN, ROWS, VECS),
            array(NWIN, ROWS, VECS),
            array(SHARES, 96, 128),
        ),
        [SMEM, VMEM, ANY, ANY, ANY, VMEM],
        [band_scratch, pltpu.VMEM((SHARES, WIDE, ROWS, VECS), BF), pltpu.SemaphoreType.DMA((3,))],
        420_000_000, 4_500_000,
        near_list, near_blocks, low, whole, high, u,
    )
    recv = exchange(sent, "y")
    low, high = halo(bottom, top)
    wide = call(widen_kernel, array(WIDE, ROWS, VECS), [VMEM] * 3, [], 0, 400_000, low, wide, high)
    wide = lax.all_gather(wide, "y", axis=0)

    cpl = call(
        coupling_kernel, cpl_out, [ANY],
        [
            pltpu.VMEM((SHARES, CPL, ROWS, VECS), BF),
            pltpu.VMEM((2 * PAIRS, RANK, 128), F32),
            pltpu.SemaphoreType.DMA,
        ],
        0, 1_000_000, held,
    )
    every = lax.all_gather(plane, "core", axis=0)
    payload = array(SHARES + 1, ROWS, VECS)
    parents, bottom, top = call(
        middle_kernel, (plane_out, payload, payload),
        [SMEM] + [VMEM] * 2 + [ANY] * 2,
        [
            rhs_scratch,
            pltpu.VMEM((2, SHARES, ROWS, VECS), BF),
            pltpu.VMEM((SHARES, 96, 128), BF),
            pltpu.SemaphoreType.DMA((3,)),
        ],
        100_000_000, 1_700_000,
        far_list, every, cpl, recv, held,
    )
    plane = exchange(parents, ("x", "z"))
    below, above = halo(bottom, top)
    every = lax.all_gather(plane, "core", axis=0)
    sent = call(
        last_kernel, array(SHARES, 128, 128), [SMEM] + [VMEM] * 2 + [ANY] * 3,
        [rhs_scratch, pltpu.VMEM((3, ROWS, VECS), BF), pltpu.SemaphoreType.DMA((3,))],
        100_000_000, 1_300_000,
        far_list, every, cpl, bottom, below, above,
    )
    coefs = exchange(sent, "y")
    plain, q = call(
        second_kernel,
        (array(LEAVES * ROWS, VECS, dtype=F32), array(LEAVES * ROWS, 4 * RANK)),
        [SMEM, VMEM] + [ANY] * 4,
        [
            band_scratch,
            pltpu.VMEM((SHARES, WIDE + GROUPS + 2, ROWS, VECS), BF),
            pltpu.SemaphoreType.DMA((4,)),
        ],
        520_000_000, 4_000_000,
        near_list, near_blocks, wide, below, held, above,
    )
    out = array(LEAVES, ROWS, VECS)
    return call(
        finish_kernel, (out, out), [VMEM] * 2 + [ANY] + [VMEM] * 2,
        [pltpu.VMEM((SHARES, 128, 128), BF), pltpu.SemaphoreType.DMA((1,))],
        100_000_000, 2_000_000,
        keep, u, coefs, plain, q,
    )


def solution(mesh):
    fine = Mesh(mesh.devices.reshape(4, 8, 2, 8), ("x", "z", "core", "y"))
    placed = (
        P(CLUS, "y", None),
        P(CLUS, None),
        P(CLUS, None),
        P(CLUS, None, "y", None),
        P(CLUS, "y", None),
        P(CLUS, None, None),
        P(CLUS, None, None, "y"),
    )
    return jax.shard_map(
        operator_twice,
        mesh=fine,
        in_specs=placed,
        out_specs=(P(CLUS, "y", None), P(CLUS, "y", None)),
        check_vma=False,
    )
```

```python
import functools

import jax
import jax.numpy as jnp
from jax import lax
from jax.experimental import pallas as pl
from jax.experimental.pallas import tpu as pltpu
from jax.sharding import Mesh
from jax.sharding import PartitionSpec as P

BF = jnp.bfloat16
F32 = jnp.float32
LEAVES = 16
ROWS = 16
PANEL = 128
RANK = 64
COLS = 32
PACK = 4
GROUPS = LEAVES // PACK
NEAR_K = 9
FAR_K = 27
NWIN = 4
SHARES = 8
PLANE = 32
PAR0 = GROUPS * ROWS
SENT = PAR0 + 32
BAS0 = LEAVES * NEAR_K * ROWS
CPL0 = BAS0 + LEAVES // 2 * ROWS
HELD = CPL0 + FAR_K * 8
HALF = FAR_K * 32
FLIGHT = 4
CLUS = ("x", "z", "core")
TOP = (((0,), (0,)), ((), ()))
ANY = pl.BlockSpec(memory_space=pl.ANY)
SMEM = pl.BlockSpec(memory_space=pltpu.SMEM)
VMEM = pl.BlockSpec(memory_space=pltpu.VMEM)


def dot(a, b):
    return jnp.dot(a, b, preferred_element_type=F32)


def dot_top(a, b):
    return lax.dot_general(a, b, TOP, preferred_element_type=F32)


def lane_group(shape):
    return lax.broadcasted_iota(jnp.int32, shape, len(shape) - 1) // COLS


def spread(rows):
    rows = rows + pltpu.roll(rows, 64, 1)
    return rows + pltpu.roll(rows, 32, 1)


def pack_parents(first, second):
    group = lane_group((32, 128))
    low = jnp.where(group == 0, first[:32], first[32:])
    high = jnp.where(group == 2, second[:32], second[32:])
    return jnp.where(group < 2, low, high).astype(BF)


def stack_kernel(near_ref, b_ref, c_ref, out_ref):
    out_ref[:BAS0] = near_ref[...].reshape(BAS0, PANEL)
    for m in range(LEAVES // 2):
        row = BAS0 + ROWS * m
        out_ref[row : row + ROWS] = jnp.concatenate([b_ref[2 * m], b_ref[2 * m + 1]], axis=1)
    both = jnp.concatenate([c_ref[0].astype(F32), c_ref[1].astype(F32)], axis=2)
    out_ref[CPL0:] = both.reshape(FAR_K * 8, 128).astype(BF)


def prepare_kernel(d_ref, b_ref, t_ref, out_ref):
    part = []
    for p in range(2):
        u = [dot(b_ref[i], t_ref[i]) for i in range(8 * p, 8 * p + 8)]
        rows = jnp.concatenate(u, axis=0).astype(BF)
        part.append(dot_top(rows, d_ref[8 * p : 8 * p + 8].reshape(8 * ROWS, 256)))
    for s in range(SHARES):
        cut = slice(COLS * s, COLS * (s + 1))
        pieces = [part[0][:32, cut], part[0][32:, cut], part[1][:32, cut], part[1][32:, cut]]
        out_ref[s, PAR0:SENT, :] = jnp.concatenate(pieces, axis=1).astype(BF)
        for g in range(GROUPS):
            pieces = [d_ref[PACK * g + l][:, cut] for l in range(PACK)]
            out_ref[s, ROWS * g : ROWS * (g + 1), :] = jnp.concatenate(pieces, axis=1)


def parent_kernel(recv_ref, out_ref, bottom_ref, top_ref):
    total = jnp.sum(recv_ref[:, PAR0:SENT, :].astype(F32), axis=0).astype(BF)
    out_ref[...] = jnp.broadcast_to(total[None], out_ref.shape)
    bottom_ref[...] = recv_ref[:, :ROWS, :]
    top_ref[...] = recv_ref[:, PAR0 - ROWS : PAR0, :]


def far_sums(far_ref, pc_ref, cpl, rhs_scr):
    side = lax.broadcasted_iota(jnp.int32, (32, 128), 1) // 64
    even = lane_group((RANK, 128)) % 2 == 0
    sums = []
    for p in range(2):
        for k in range(FAR_K):
            parent = far_ref[p, k]
            tile = pc_ref[(parent // 2) % 2, parent // 4]
            rhs_scr[32 * k : 32 * (k + 1), :] = jnp.where(side == parent % 2, tile, jnp.zeros_like(tile))
        rhs = rhs_scr[...]
        acc0 = dot(cpl[0][RANK * p : RANK * (p + 1)], rhs)
        acc1 = dot(cpl[1][RANK * p : RANK * (p + 1)], rhs)
        sums.append(spread(jnp.where(even, acc0, acc1)).astype(BF).astype(F32))
    return sums


def far_field(u, coef):
    group = lane_group((RANK, 128))
    blocks = [jnp.where(group == l, coef, 0.0) for l in range(PACK)]
    return dot(u, jnp.concatenate(blocks, axis=0).astype(BF))


def near_copies(w_ref, near_scr, sems, leaves):
    size = NEAR_K * ROWS
    return [
        pltpu.make_async_copy(w_ref.at[:, pl.ds(size * i, size), :], near_scr.at[n], sems.at[n])
        for n, i in enumerate(leaves)
    ]


def unpack(start, tiles, v_scr):
    for n, tile in enumerate(tiles):
        for l in range(PACK):
            v_scr[PACK * (start + n) + l] = tile[:, COLS * l : COLS * (l + 1)]


def near_leaf(i, n, idx_ref, near_scr, v_scr):
    parts = [near_scr[n, :, ROWS * k : ROWS * (k + 1), :].reshape(PANEL, PANEL) for k in range(NEAR_K)]
    rhs = jnp.concatenate([v_scr[idx_ref[i, k]] for k in range(NEAR_K)], axis=0)
    return dot(jnp.concatenate(parts, axis=1), rhs)


def first_kernel(
    far_ref, idx_ref, pc_ref, w_ref, t_ref, recv_ref, lo_ref, hi_ref,
    out_ref, par_ref, bottom_ref, top_ref, cpl_ref, u_ref,
    near_scr, own_scr, c_scr, rhs_scr, v_scr, sems, own_sem,
):
    own = pltpu.make_async_copy(w_ref.at[:, pl.ds(BAS0, HELD - BAS0), :], own_scr, own_sem)
    own.start()
    tiles = [lo_ref[...]] + [recv_ref[:, ROWS * g : ROWS * (g + 1), :] for g in range(GROUPS)] + [hi_ref[...]]
    unpack(0, [tile.reshape(PANEL, 128) for tile in tiles], v_scr)
    own.wait()
    copies = near_copies(w_ref, near_scr, sems, range(LEAVES))
    for copy in copies:
        copy.start()
    for y in range(SHARES):
        rows = own_scr[y, CPL0 - BAS0 :, :].astype(F32).reshape(FAR_K, 8, 128)
        c_scr[:, 8 * y : 8 * y + 8, :] = rows
    cpl = [c_scr[:, 32 * h : 32 * (h + 1), :].reshape(HALF, 128).T.astype(BF) for h in range(2)]
    for h in range(2):
        cpl_ref[h] = cpl[h]
    zero = jnp.zeros((RANK, RANK), BF)
    for m in range(LEAVES // 2):
        rows = own_scr[:, ROWS * m : ROWS * (m + 1), :].reshape(PANEL, 128)
        upper = jnp.concatenate([t_ref[2 * m], zero], axis=1)
        lower = jnp.concatenate([zero, t_ref[2 * m + 1]], axis=1)
        pair = dot(rows, jnp.concatenate([upper, lower], axis=0)).astype(BF)
        u_ref[m // 2, :, 128 * (m % 2) : 128 * (m % 2 + 1)] = pair
    coef = far_sums(far_ref, pc_ref, cpl, rhs_scr)
    group = lane_group((RANK, 128))
    parents = [jnp.zeros((RANK, 128), F32), jnp.zeros((RANK, 128), F32)]
    for g in range(GROUPS):
        u = u_ref[g]
        cols = []
        for i in range(PACK * g, PACK * (g + 1)):
            copies[i].wait()
            cols.append(near_leaf(i, i, idx_ref, near_scr, v_scr))
        res = (jnp.concatenate(cols, axis=1) + far_field(u, coef[g // 2])).astype(BF)
        tile = res.reshape(SHARES, ROWS, 128)
        out_ref[:, g] = tile
        if g == 0:
            bottom_ref[...] = tile
        if g == GROUPS - 1:
            top_ref[...] = tile
        x = dot_top(u, res)
        for l in range(PACK):
            parents[g // 2] += jnp.where(group == l, x[RANK * l : RANK * (l + 1)], 0.0)
    packed = pack_parents(spread(parents[0]), spread(parents[1]))
    par_ref[...] = jnp.broadcast_to(packed[None], par_ref.shape)


def near_kernel(groups, idx_ref, w_ref, *refs):
    *tile_refs, out_ref, near_scr, v_scr, sems = refs
    leaves = [i for g in groups for i in range(PACK * g, PACK * (g + 1))]
    copies = near_copies(w_ref, near_scr, sems, leaves)
    for copy in copies[:FLIGHT]:
        copy.start()
    tiles = [tile_refs[0][:, g] for g in range(GROUPS)]
    unpack(1, [tile.reshape(PANEL, 128) for tile in tiles], v_scr)
    if len(tile_refs) > 1:
        unpack(0, [tile_refs[1][...].reshape(PANEL, 128)], v_scr)
        unpack(GROUPS + 1, [tile_refs[2][...].reshape(PANEL, 128)], v_scr)
    cols = []
    for n, i in enumerate(leaves):
        copies[n].wait()
        if n + FLIGHT < len(leaves):
            copies[n + FLIGHT].start()
        cols.append(near_leaf(i, n, idx_ref, near_scr, v_scr))
    for n in range(len(groups)):
        out_ref[n] = jnp.concatenate(cols[PACK * n : PACK * (n + 1)], axis=1)


def last_kernel(far_ref, pc_ref, cpl_ref, u_ref, mid_ref, edge_ref, own_ref, out_ref, rhs_scr):
    coef = far_sums(far_ref, pc_ref, (cpl_ref[0], cpl_ref[1]), rhs_scr)
    for g in range(GROUPS):
        near = mid_ref[g - 1] if 0 < g < GROUPS - 1 else edge_ref[g // (GROUPS - 1)]
        res = (near + far_field(u_ref[g], coef[g // 2])).astype(BF)
        out_ref[:, 0, g] = own_ref[:, g]
        out_ref[:, 1, g] = res.reshape(SHARES, ROWS, 128)


def finish_kernel(recv_ref, first_ref, second_ref):
    for o, ref in enumerate((first_ref, second_ref)):
        for g in range(GROUPS):
            for b in range(2):
                tiles = [recv_ref[PACK * b + s, o, g] for s in range(PACK)]
                for l in range(PACK):
                    cut = slice(COLS * l, COLS * (l + 1))
                    ref[PACK * g + l, :, 128 * b : 128 * (b + 1)] = jnp.concatenate([t[:, cut] for t in tiles], axis=1)


def array(*shape, dtype=BF):
    return jax.ShapeDtypeStruct(shape, dtype)


def call(kernel, outs, ins, scratch, flops, nbytes, *operands):
    single = not isinstance(outs, tuple)
    return pl.pallas_call(
        kernel,
        out_shape=outs,
        in_specs=ins,
        out_specs=VMEM if single else (VMEM,) * len(outs),
        scratch_shapes=scratch,
        cost_estimate=pl.CostEstimate(flops=flops, bytes_accessed=nbytes, transcendentals=0),
    )(*operands)


def exchange(values):
    return lax.all_to_all(values, ("x", "z"), 0, 0)


def halo(bottom, top):
    count = 64
    forward = [(i, i + 1) for i in range(count - 1)]
    backward = [(target, source) for source, target in forward]
    return lax.ppermute(top, CLUS, forward), lax.ppermute(bottom, CLUS, backward)


def operator_twice(density, near_list, far_list, near_blocks, basis, transfer, coupling):
    share = array(SHARES, ROWS, 128)
    spread_out = array(PLANE, 32, 128)
    near_scratch = pltpu.VMEM((LEAVES, SHARES, NEAR_K * ROWS, PANEL), BF)
    vec_scratch = pltpu.VMEM((LEAVES + 2 * NWIN, PANEL, COLS), BF)
    rhs_scratch = pltpu.VMEM((HALF, 128), BF)
    near_sems = pltpu.SemaphoreType.DMA((LEAVES,))

    mine = call(
        stack_kernel, array(HELD, PANEL), [VMEM] * 3, [], 0, 1_400_000,
        near_blocks, basis, jnp.swapaxes(coupling, 2, 3),
    )
    held = lax.all_gather(mine, "y", axis=0)
    near_idx = near_list - (lax.axis_index(CLUS) * LEAVES - NWIN)
    near_idx = jnp.clip(near_idx, 0, LEAVES + 2 * NWIN - 1)
    sent = call(
        prepare_kernel, array(SHARES, SENT, 128), [VMEM] * 3, [], 40_000_000, 500_000,
        density, basis, transfer,
    )
    recv = lax.all_to_all(sent, "y", 0, 0)
    parents, bottom, top = call(
        parent_kernel, (spread_out, share, share), [VMEM], [], 100_000, 500_000, recv
    )
    every = lax.all_gather(exchange(parents), "core", axis=0)
    low, high = halo(bottom, top)
    first, parents, bottom, top, cpl, u = call(
        first_kernel,
        (
            array(SHARES, GROUPS, ROWS, 128), spread_out, share, share,
            array(2, 2 * RANK, HALF), array(GROUPS, PANEL, PACK * RANK),
        ),
        [SMEM, SMEM, VMEM, ANY] + [VMEM] * 4,
        [
            near_scratch,
            pltpu.VMEM((SHARES, HELD - BAS0, 128), BF),
            pltpu.VMEM((FAR_K, RANK, 128), F32),
            rhs_scratch,
            vec_scratch,
            near_sems,
            pltpu.SemaphoreType.DMA,
        ],
        400_000_000, 8_000_000,
        far_list, near_idx, every, held, transfer, recv, low, high,
    )
    plane = exchange(parents)
    low, high = halo(bottom, top)
    half = array(GROUPS // 2, PANEL, 128, dtype=F32)
    half_scratch = [
        pltpu.VMEM((LEAVES // 2, SHARES, NEAR_K * ROWS, PANEL), BF),
        vec_scratch,
        pltpu.SemaphoreType.DMA((LEAVES // 2,)),
    ]
    mid = call(
        functools.partial(near_kernel, (1, 2)), half, [SMEM, ANY, VMEM],
        half_scratch, 150_000_000, 3_000_000,
        near_idx, held, first,
    )
    edge = call(
        functools.partial(near_kernel, (0, 3)), half, [SMEM, ANY] + [VMEM] * 3,
        half_scratch, 150_000_000, 3_000_000,
        near_idx, held, first, low, high,
    )
    every = lax.all_gather(plane, "core", axis=0)
    sent = call(
        last_kernel, array(SHARES, 2, GROUPS, ROWS, 128), [SMEM] + [VMEM] * 6,
        [rhs_scratch], 100_000_000, 2_000_000,
        far_list, every, cpl, u, mid, edge, first,
    )
    out = array(LEAVES, ROWS, 256)
    return call(finish_kernel, (out, out), [VMEM], [], 0, 600_000, lax.all_to_all(sent, "y", 0, 0))


def solution(mesh):
    fine = Mesh(mesh.devices.reshape(4, 8, 2, 8), ("x", "z", "core", "y"))
    placed = (
        P(CLUS, "y", None),
        P(CLUS, None),
        P(CLUS, None),
        P(CLUS, None, "y", None),
        P(CLUS, "y", None),
        P(CLUS, None, None),
        P(CLUS, None, None, "y"),
    )
    return jax.shard_map(
        operator_twice,
        mesh=fine,
        in_specs=placed,
        out_specs=(P(CLUS, "y", None), P(CLUS, "y", None)),
        check_vma=False,
    )
```

```python
import jax
import jax.numpy as jnp
from jax import lax
from jax.experimental import pallas as pl
from jax.experimental.pallas import tpu as pltpu
from jax.sharding import Mesh
from jax.sharding import PartitionSpec as P

BF = jnp.bfloat16
F32 = jnp.float32
LEAVES = 16
ROWS = 16
PANEL = 128
RANK = 64
COLS = 32
PACK = 4
GROUPS = LEAVES // PACK
NEAR_K = 9
FAR_K = 27
NWIN = 4
SHARES = 8
PLANE = 32
PAR0 = GROUPS * ROWS
SENT = PAR0 + 32
BAS0 = LEAVES * NEAR_K * ROWS
CPL0 = BAS0 + LEAVES // 2 * ROWS
HELD = CPL0 + FAR_K * 8
HALF = FAR_K * 32
BATCH = 8
CLUS = ("x", "z", "core")
TOP = (((0,), (0,)), ((), ()))
ANY = pl.BlockSpec(memory_space=pl.ANY)
SMEM = pl.BlockSpec(memory_space=pltpu.SMEM)
VMEM = pl.BlockSpec(memory_space=pltpu.VMEM)


def dot(a, b):
    return jnp.dot(a, b, preferred_element_type=F32)


def dot_top(a, b):
    return lax.dot_general(a, b, TOP, preferred_element_type=F32)


def lane_group(shape):
    return lax.broadcasted_iota(jnp.int32, shape, len(shape) - 1) // COLS


def spread(rows):
    rows = rows + pltpu.roll(rows, 64, 1)
    return rows + pltpu.roll(rows, 32, 1)


def pack_parents(first, second):
    group = lane_group((32, 128))
    low = jnp.where(group == 0, first[:32], first[32:])
    high = jnp.where(group == 2, second[:32], second[32:])
    return jnp.where(group < 2, low, high).astype(BF)


def fetch(pairs, sems):
    moves = [pltpu.make_async_copy(src, dst, sems.at[n]) for n, (src, dst) in enumerate(pairs)]
    for move in moves:
        move.start()
    return moves


def stack_kernel(near_ref, b_ref, c_ref, out_ref):
    out_ref[:BAS0] = near_ref[...].reshape(BAS0, PANEL)
    for m in range(LEAVES // 2):
        row = BAS0 + ROWS * m
        out_ref[row : row + ROWS] = jnp.concatenate([b_ref[2 * m], b_ref[2 * m + 1]], axis=1)
    both = jnp.concatenate([c_ref[0].astype(F32), c_ref[1].astype(F32)], axis=2)
    out_ref[CPL0:] = both.reshape(FAR_K * 8, 128).astype(BF)


def prepare_kernel(d_ref, b_ref, t_ref, out_ref):
    part = []
    for p in range(2):
        u = [dot(b_ref[i], t_ref[i]) for i in range(8 * p, 8 * p + 8)]
        rows = jnp.concatenate(u, axis=0).astype(BF)
        part.append(dot_top(rows, d_ref[8 * p : 8 * p + 8].reshape(8 * ROWS, 256)))
    for s in range(SHARES):
        cut = slice(COLS * s, COLS * (s + 1))
        pieces = [part[0][:32, cut], part[0][32:, cut], part[1][:32, cut], part[1][32:, cut]]
        out_ref[s, PAR0:SENT, :] = jnp.concatenate(pieces, axis=1).astype(BF)
        for g in range(GROUPS):
            pieces = [d_ref[PACK * g + l][:, cut] for l in range(PACK)]
            out_ref[s, ROWS * g : ROWS * (g + 1), :] = jnp.concatenate(pieces, axis=1)


def parent_kernel(recv_ref, out_ref, bottom_ref, top_ref):
    total = jnp.sum(recv_ref[:, PAR0:SENT, :].astype(F32), axis=0).astype(BF)
    out_ref[...] = jnp.broadcast_to(total[None], out_ref.shape)
    bottom_ref[...] = recv_ref[:, :ROWS, :]
    top_ref[...] = recv_ref[:, PAR0 - ROWS : PAR0, :]


def far_sums(far_ref, pc_ref, cpl, rhs_scr):
    side = lax.broadcasted_iota(jnp.int32, (32, 128), 1) // 64
    even = lane_group((RANK, 128)) % 2 == 0
    sums = []
    for p in range(2):
        for k in range(FAR_K):
            parent = far_ref[p, k]
            tile = pc_ref[(parent // 2) % 2, parent // 4]
            rhs_scr[32 * k : 32 * (k + 1), :] = jnp.where(side == parent % 2, tile, jnp.zeros_like(tile))
        rhs = rhs_scr[...]
        acc0 = dot(cpl[0][RANK * p : RANK * (p + 1)], rhs)
        acc1 = dot(cpl[1][RANK * p : RANK * (p + 1)], rhs)
        sums.append(spread(jnp.where(even, acc0, acc1)).astype(BF).astype(F32))
    return sums


def far_field(u, coef):
    group = lane_group((RANK, 128))
    blocks = [jnp.where(group == l, coef, 0.0) for l in range(PACK)]
    return dot(u, jnp.concatenate(blocks, axis=0).astype(BF))


def near_copies(w_ref, near_scr, sems, leaves):
    size = NEAR_K * ROWS
    return [
        pltpu.make_async_copy(w_ref.at[:, pl.ds(size * i, size), :], near_scr.at[n], sems.at[n])
        for n, i in enumerate(leaves)
    ]


def unpack(start, tiles, v_scr):
    for n, tile in enumerate(tiles):
        for l in range(PACK):
            v_scr[PACK * (start + n) + l] = tile[:, COLS * l : COLS * (l + 1)]


def near_field(idx_ref, copies, near_scr, v_scr):
    for start in range(0, LEAVES, BATCH):
        for i in range(start, start + BATCH):
            copies[i].wait()
        cols = []
        for i in range(start, start + BATCH):
            parts = [near_scr[i, :, ROWS * k : ROWS * (k + 1), :].reshape(PANEL, PANEL) for k in range(NEAR_K)]
            rhs = jnp.concatenate([v_scr[idx_ref[i, k]] for k in range(NEAR_K)], axis=0)
            cols.append(dot(jnp.concatenate(parts, axis=1), rhs))
        for n in range(0, BATCH, PACK):
            yield jnp.concatenate(cols[n : n + PACK], axis=1)


def first_kernel(
    far_ref, idx_ref, pc_in, w_ref, t_in, recv_ref, lo_ref, hi_ref,
    out_ref, par_ref, bottom_ref, top_ref, cpl_out, u_out,
    near_scr, own_scr, c_scr, rhs_scr, v_scr, cpl_ref, u_ref, pc_ref, t_ref, sems, own_sem, side_sems,
):
    own = pltpu.make_async_copy(w_ref.at[:, pl.ds(BAS0, HELD - BAS0), :], own_scr, own_sem)
    own.start()
    sources = fetch(((t_in, t_ref), (pc_in, pc_ref)), side_sems)
    copies = near_copies(w_ref, near_scr, sems, range(LEAVES))
    for copy in copies:
        copy.start()
    tiles = [lo_ref[...]] + [recv_ref[:, ROWS * g : ROWS * (g + 1), :] for g in range(GROUPS)] + [hi_ref[...]]
    unpack(0, [tile.reshape(PANEL, 128) for tile in tiles], v_scr)
    own.wait()
    for source in sources:
        source.wait()
    for y in range(SHARES):
        rows = own_scr[y, CPL0 - BAS0 :, :].astype(F32).reshape(FAR_K, 8, 128)
        c_scr[:, 8 * y : 8 * y + 8, :] = rows
    cpl = [c_scr[:, 32 * h : 32 * (h + 1), :].reshape(HALF, 128).T.astype(BF) for h in range(2)]
    for h in range(2):
        cpl_ref[h] = cpl[h]
    zero = jnp.zeros((RANK, RANK), BF)
    for m in range(LEAVES // 2):
        rows = own_scr[:, ROWS * m : ROWS * (m + 1), :].reshape(PANEL, 128)
        upper = jnp.concatenate([t_ref[2 * m], zero], axis=1)
        lower = jnp.concatenate([zero, t_ref[2 * m + 1]], axis=1)
        pair = dot(rows, jnp.concatenate([upper, lower], axis=0)).astype(BF)
        u_ref[m // 2, :, 128 * (m % 2) : 128 * (m % 2 + 1)] = pair
    sides = fetch(((cpl_ref, cpl_out), (u_ref, u_out)), side_sems)
    coef = far_sums(far_ref, pc_ref, cpl, rhs_scr)
    group = lane_group((RANK, 128))
    parents = [jnp.zeros((RANK, 128), F32), jnp.zeros((RANK, 128), F32)]
    for g, near in enumerate(near_field(idx_ref, copies, near_scr, v_scr)):
        u = u_ref[g]
        res = (near + far_field(u, coef[g // 2])).astype(BF)
        tile = res.reshape(SHARES, ROWS, 128)
        out_ref[:, g] = tile
        if g == 0:
            bottom_ref[...] = tile
        if g == GROUPS - 1:
            top_ref[...] = tile
        x = dot_top(u, res)
        for l in range(PACK):
            parents[g // 2] += jnp.where(group == l, x[RANK * l : RANK * (l + 1)], 0.0)
    packed = pack_parents(spread(parents[0]), spread(parents[1]))
    par_ref[...] = jnp.broadcast_to(packed[None], par_ref.shape)
    for side in sides:
        side.wait()


def near_kernel(idx_ref, w_ref, vec_ref, lo_ref, hi_ref, out_ref, near_scr, v_scr, sems):
    copies = near_copies(w_ref, near_scr, sems, range(LEAVES))
    for copy in copies:
        copy.start()
    tiles = [lo_ref[...]] + [vec_ref[:, g] for g in range(GROUPS)] + [hi_ref[...]]
    unpack(0, [tile.reshape(PANEL, 128) for tile in tiles], v_scr)
    for g, near in enumerate(near_field(idx_ref, copies, near_scr, v_scr)):
        out_ref[g] = near


def last_kernel(far_ref, pc_ref, cpl_ref, u_ref, near_ref, own_ref, out_ref, rhs_scr):
    coef = far_sums(far_ref, pc_ref, (cpl_ref[0], cpl_ref[1]), rhs_scr)
    for g in range(GROUPS):
        res = (near_ref[g] + far_field(u_ref[g], coef[g // 2])).astype(BF)
        out_ref[:, 0, g] = own_ref[:, g]
        out_ref[:, 1, g] = res.reshape(SHARES, ROWS, 128)


def finish_kernel(recv_ref, first_ref, second_ref):
    for o, ref in enumerate((first_ref, second_ref)):
        for g in range(GROUPS):
            for b in range(2):
                tiles = [recv_ref[PACK * b + s, o, g] for s in range(PACK)]
                for l in range(PACK):
                    cut = slice(COLS * l, COLS * (l + 1))
                    ref[PACK * g + l, :, 128 * b : 128 * (b + 1)] = jnp.concatenate([t[:, cut] for t in tiles], axis=1)


def array(*shape, dtype=BF):
    return jax.ShapeDtypeStruct(shape, dtype)


def call(kernel, outs, ins, scratch, flops, nbytes, *operands, sides=0):
    single = not isinstance(outs, tuple)
    return pl.pallas_call(
        kernel,
        out_shape=outs,
        in_specs=ins,
        out_specs=VMEM if single else (VMEM,) * (len(outs) - sides) + (ANY,) * sides,
        scratch_shapes=scratch,
        cost_estimate=pl.CostEstimate(flops=flops, bytes_accessed=nbytes, transcendentals=0),
    )(*operands)


def exchange(values):
    return lax.all_to_all(values, ("x", "z"), 0, 0)


def halo(bottom, top):
    count = 64
    forward = [(i, i + 1) for i in range(count - 1)]
    backward = [(target, source) for source, target in forward]
    return lax.ppermute(top, CLUS, forward), lax.ppermute(bottom, CLUS, backward)


def operator_twice(density, near_list, far_list, near_blocks, basis, transfer, coupling):
    share = array(SHARES, ROWS, 128)
    spread_out = array(PLANE, 32, 128)
    near_scratch = pltpu.VMEM((LEAVES, SHARES, NEAR_K * ROWS, PANEL), BF)
    vec_scratch = pltpu.VMEM((LEAVES + 2 * NWIN, PANEL, COLS), BF)
    rhs_scratch = pltpu.VMEM((HALF, 128), BF)
    near_sems = pltpu.SemaphoreType.DMA((LEAVES,))

    mine = call(
        stack_kernel, array(HELD, PANEL), [VMEM] * 3, [], 0, 1_400_000,
        near_blocks, basis, jnp.swapaxes(coupling, 2, 3),
    )
    held = lax.all_gather(mine, "y", axis=0)
    near_idx = near_list - (lax.axis_index(CLUS) * LEAVES - NWIN)
    near_idx = jnp.clip(near_idx, 0, LEAVES + 2 * NWIN - 1)
    sent = call(
        prepare_kernel, array(SHARES, SENT, 128), [VMEM] * 3, [], 40_000_000, 500_000,
        density, basis, transfer,
    )
    recv = lax.all_to_all(sent, "y", 0, 0)
    parents, bottom, top = call(
        parent_kernel, (spread_out, share, share), [VMEM], [], 100_000, 500_000, recv
    )
    every = lax.all_gather(exchange(parents), "core", axis=0)
    low, high = halo(bottom, top)
    first, parents, bottom, top, cpl, u = call(
        first_kernel,
        (
            array(SHARES, GROUPS, ROWS, 128), spread_out, share, share,
            array(2, 2 * RANK, HALF), array(GROUPS, PANEL, PACK * RANK),
        ),
        [SMEM, SMEM] + [ANY] * 3 + [VMEM] * 3,
        [
            near_scratch,
            pltpu.VMEM((SHARES, HELD - BAS0, 128), BF),
            pltpu.VMEM((FAR_K, RANK, 128), F32),
            rhs_scratch,
            vec_scratch,
            pltpu.VMEM((2, 2 * RANK, HALF), BF),
            pltpu.VMEM((GROUPS, PANEL, PACK * RANK), BF),
            pltpu.VMEM((2, PLANE, 32, 128), BF),
            pltpu.VMEM((LEAVES, RANK, RANK), BF),
            near_sems,
            pltpu.SemaphoreType.DMA,
            pltpu.SemaphoreType.DMA((2,)),
        ],
        400_000_000, 8_000_000,
        far_list, near_idx, every, held, transfer, recv, low, high,
        sides=2,
    )
    plane = exchange(parents)
    low, high = halo(bottom, top)
    near = call(
        near_kernel, array(GROUPS, PANEL, 128, dtype=F32), [SMEM, ANY] + [VMEM] * 3,
        [near_scratch, vec_scratch, near_sems], 300_000_000, 6_000_000,
        near_idx, held, first, low, high,
    )
    every = lax.all_gather(plane, "core", axis=0)
    sent = call(
        last_kernel, array(SHARES, 2, GROUPS, ROWS, 128), [SMEM] + [VMEM] * 5,
        [rhs_scratch], 100_000_000, 2_000_000,
        far_list, every, cpl, u, near, first,
    )
    out = array(LEAVES, ROWS, 256)
    return call(finish_kernel, (out, out), [VMEM], [], 0, 600_000, lax.all_to_all(sent, "y", 0, 0))


def solution(mesh):
    fine = Mesh(mesh.devices.reshape(4, 8, 2, 8), ("x", "z", "core", "y"))
    placed = (
        P(CLUS, "y", None),
        P(CLUS, None),
        P(CLUS, None),
        P(CLUS, None, "y", None),
        P(CLUS, "y", None),
        P(CLUS, None, None),
        P(CLUS, None, None, "y"),
    )
    return jax.shard_map(
        operator_twice,
        mesh=fine,
        in_specs=placed,
        out_specs=(P(CLUS, "y", None), P(CLUS, "y", None)),
        check_vma=False,
    )
```

```python
import jax
import jax.numpy as jnp
from jax import lax
from jax.experimental import pallas as pl
from jax.experimental.pallas import tpu as pltpu
from jax.sharding import Mesh
from jax.sharding import PartitionSpec as P

BF = jnp.bfloat16
F32 = jnp.float32
LEAVES = 16
ROWS = 16
PANEL = 128
RANK = 64
COLS = 32
PACK = 4
GROUPS = LEAVES // PACK
NEAR_K = 9
FAR_K = 27
NWIN = 4
SHARES = 8
PLANE = 32
PAR0 = GROUPS * ROWS
SENT = PAR0 + 32
BAS0 = LEAVES * NEAR_K * ROWS
CPL0 = BAS0 + LEAVES // 2 * ROWS
HELD = CPL0 + FAR_K * 8
HALF = FAR_K * 32
BATCH = 8
CLUS = ("x", "z", "core")
TOP = (((0,), (0,)), ((), ()))
ANY = pl.BlockSpec(memory_space=pl.ANY)
SMEM = pl.BlockSpec(memory_space=pltpu.SMEM)
VMEM = pl.BlockSpec(memory_space=pltpu.VMEM)


def dot(a, b):
    return jnp.dot(a, b, preferred_element_type=F32)


def dot_top(a, b):
    return lax.dot_general(a, b, TOP, preferred_element_type=F32)


def lane_group(shape):
    return lax.broadcasted_iota(jnp.int32, shape, len(shape) - 1) // COLS


def spread(rows):
    rows = rows + pltpu.roll(rows, 64, 1)
    return rows + pltpu.roll(rows, 32, 1)


def pack_parents(first, second):
    group = lane_group((32, 128))
    low = jnp.where(group == 0, first[:32], first[32:])
    high = jnp.where(group == 2, second[:32], second[32:])
    return jnp.where(group < 2, low, high).astype(BF)


def fetch(pairs, sems):
    moves = [pltpu.make_async_copy(src, dst, sems.at[n]) for n, (src, dst) in enumerate(pairs)]
    for move in moves:
        move.start()
    return moves


def stack_kernel(near_ref, b_ref, c_ref, out_ref):
    out_ref[:BAS0] = near_ref[...].reshape(BAS0, PANEL)
    for m in range(LEAVES // 2):
        row = BAS0 + ROWS * m
        out_ref[row : row + ROWS] = jnp.concatenate([b_ref[2 * m], b_ref[2 * m + 1]], axis=1)
    both = jnp.concatenate([c_ref[0].astype(F32), c_ref[1].astype(F32)], axis=2)
    out_ref[CPL0:] = both.reshape(FAR_K * 8, 128).astype(BF)


def prepare_kernel(d_ref, b_ref, t_ref, out_ref):
    part = []
    for p in range(2):
        u = [dot(b_ref[i], t_ref[i]) for i in range(8 * p, 8 * p + 8)]
        rows = jnp.concatenate(u, axis=0).astype(BF)
        part.append(dot_top(rows, d_ref[8 * p : 8 * p + 8].reshape(8 * ROWS, 256)))
    for s in range(SHARES):
        cut = slice(COLS * s, COLS * (s + 1))
        pieces = [part[0][:32, cut], part[0][32:, cut], part[1][:32, cut], part[1][32:, cut]]
        out_ref[s, PAR0:SENT, :] = jnp.concatenate(pieces, axis=1).astype(BF)
        for g in range(GROUPS):
            pieces = [d_ref[PACK * g + l][:, cut] for l in range(PACK)]
            out_ref[s, ROWS * g : ROWS * (g + 1), :] = jnp.concatenate(pieces, axis=1)


def parent_kernel(recv_ref, out_ref, bottom_ref, top_ref):
    total = jnp.sum(recv_ref[:, PAR0:SENT, :].astype(F32), axis=0).astype(BF)
    out_ref[...] = jnp.broadcast_to(total[None], out_ref.shape)
    bottom_ref[...] = recv_ref[:, :ROWS, :]
    top_ref[...] = recv_ref[:, PAR0 - ROWS : PAR0, :]


def far_sums(far_ref, pc_ref, cpl, rhs_scr):
    side = lax.broadcasted_iota(jnp.int32, (32, 128), 1) // 64
    even = lane_group((RANK, 128)) % 2 == 0
    sums = []
    for p in range(2):
        for k in range(FAR_K):
            parent = far_ref[p, k]
            tile = pc_ref[(parent // 2) % 2, parent // 4]
            rhs_scr[32 * k : 32 * (k + 1), :] = jnp.where(side == parent % 2, tile, jnp.zeros_like(tile))
        rhs = rhs_scr[...]
        rows = slice(RANK * p, RANK * (p + 1))
        acc = dot(jnp.concatenate([cpl[0][rows], cpl[1][rows]], axis=0), rhs)
        sums.append(spread(jnp.where(even, acc[:RANK], acc[RANK:])).astype(BF).astype(F32))
    return sums


def far_field(u, coef):
    group = lane_group((RANK, 128))
    blocks = [jnp.where(group == l, coef, 0.0) for l in range(PACK)]
    return dot(u, jnp.concatenate(blocks, axis=0).astype(BF))


def near_copies(w_ref, near_scr, sems, leaves):
    size = NEAR_K * ROWS
    return [
        pltpu.make_async_copy(w_ref.at[:, pl.ds(size * i, size), :], near_scr.at[n], sems.at[n])
        for n, i in enumerate(leaves)
    ]


def unpack(start, tiles, v_scr):
    for n, tile in enumerate(tiles):
        for l in range(PACK):
            v_scr[PACK * (start + n) + l] = tile[:, COLS * l : COLS * (l + 1)]


def near_field(idx_ref, copies, near_scr, v_scr):
    for start in range(0, LEAVES, BATCH):
        for i in range(start, start + BATCH):
            copies[i].wait()
        cols = []
        for i in range(start, start + BATCH):
            parts = [near_scr[i, :, ROWS * k : ROWS * (k + 1), :].reshape(PANEL, PANEL) for k in range(NEAR_K)]
            rhs = jnp.concatenate([v_scr[idx_ref[i, k]] for k in range(NEAR_K)], axis=0)
            cols.append(dot(jnp.concatenate(parts, axis=1), rhs))
        for n in range(0, BATCH, PACK):
            yield jnp.concatenate(cols[n : n + PACK], axis=1)


def first_kernel(
    far_ref, idx_ref, pc_in, w_ref, t_in, recv_ref, lo_ref, hi_ref,
    out_ref, par_ref, bottom_ref, top_ref, cpl_out, u_out,
    near_scr, own_scr, c_scr, rhs_scr, v_scr, cpl_ref, u_ref, pc_ref, t_ref, sems, own_sem, side_sems,
):
    own = pltpu.make_async_copy(w_ref.at[:, pl.ds(BAS0, HELD - BAS0), :], own_scr, own_sem)
    own.start()
    sources = fetch(((t_in, t_ref), (pc_in, pc_ref)), side_sems)
    copies = near_copies(w_ref, near_scr, sems, range(LEAVES))
    tiles = [lo_ref[...]] + [recv_ref[:, ROWS * g : ROWS * (g + 1), :] for g in range(GROUPS)] + [hi_ref[...]]
    unpack(0, [tile.reshape(PANEL, 128) for tile in tiles], v_scr)
    own.wait()
    for source in sources:
        source.wait()
    for copy in copies[:BATCH]:
        copy.start()
    for y in range(SHARES):
        rows = own_scr[y, CPL0 - BAS0 :, :].astype(F32).reshape(FAR_K, 8, 128)
        c_scr[:, 8 * y : 8 * y + 8, :] = rows
    cpl = [c_scr[:, 32 * h : 32 * (h + 1), :].reshape(HALF, 128).T.astype(BF) for h in range(2)]
    for h in range(2):
        cpl_ref[h] = cpl[h]
    zero = jnp.zeros((RANK, RANK), BF)
    for m in range(LEAVES // 2):
        rows = own_scr[:, ROWS * m : ROWS * (m + 1), :].reshape(PANEL, 128)
        upper = jnp.concatenate([t_ref[2 * m], zero], axis=1)
        lower = jnp.concatenate([zero, t_ref[2 * m + 1]], axis=1)
        pair = dot(rows, jnp.concatenate([upper, lower], axis=0)).astype(BF)
        u_ref[m // 2, :, 128 * (m % 2) : 128 * (m % 2 + 1)] = pair
    for copy in copies[BATCH:]:
        copy.start()
    sides = fetch(((cpl_ref, cpl_out), (u_ref, u_out)), side_sems)
    coef = far_sums(far_ref, pc_ref, cpl, rhs_scr)
    group = lane_group((RANK, 128))
    parents = [jnp.zeros((RANK, 128), F32), jnp.zeros((RANK, 128), F32)]
    for g, near in enumerate(near_field(idx_ref, copies, near_scr, v_scr)):
        u = u_ref[g]
        res = (near + far_field(u, coef[g // 2])).astype(BF)
        tile = res.reshape(SHARES, ROWS, 128)
        out_ref[:, g] = tile
        if g == 0:
            bottom_ref[...] = tile
        if g == GROUPS - 1:
            top_ref[...] = tile
        x = dot_top(u, res)
        for l in range(PACK):
            parents[g // 2] += jnp.where(group == l, x[RANK * l : RANK * (l + 1)], 0.0)
    packed = pack_parents(spread(parents[0]), spread(parents[1]))
    par_ref[...] = jnp.broadcast_to(packed[None], par_ref.shape)
    for side in sides:
        side.wait()


def near_kernel(idx_ref, w_ref, vec_ref, lo_ref, hi_ref, out_ref, near_scr, v_scr, sems):
    copies = near_copies(w_ref, near_scr, sems, range(LEAVES))
    for copy in copies[:BATCH]:
        copy.start()
    tiles = [lo_ref[...]] + [vec_ref[:, g] for g in range(GROUPS)] + [hi_ref[...]]
    unpack(0, [tile.reshape(PANEL, 128) for tile in tiles], v_scr)
    for copy in copies[BATCH:]:
        copy.start()
    for g, near in enumerate(near_field(idx_ref, copies, near_scr, v_scr)):
        out_ref[g] = near


def last_kernel(far_ref, pc_ref, cpl_ref, u_ref, near_ref, own_ref, out_ref, rhs_scr):
    coef = far_sums(far_ref, pc_ref, (cpl_ref[0], cpl_ref[1]), rhs_scr)
    for g in range(GROUPS):
        res = (near_ref[g] + far_field(u_ref[g], coef[g // 2])).astype(BF)
        out_ref[:, 0, g] = own_ref[:, g]
        out_ref[:, 1, g] = res.reshape(SHARES, ROWS, 128)


def finish_kernel(recv_ref, first_ref, second_ref):
    for o, ref in enumerate((first_ref, second_ref)):
        for g in range(GROUPS):
            for b in range(2):
                tiles = [recv_ref[PACK * b + s, o, g] for s in range(PACK)]
                for l in range(PACK):
                    cut = slice(COLS * l, COLS * (l + 1))
                    ref[PACK * g + l, :, 128 * b : 128 * (b + 1)] = jnp.concatenate([t[:, cut] for t in tiles], axis=1)


def array(*shape, dtype=BF):
    return jax.ShapeDtypeStruct(shape, dtype)


def call(kernel, outs, ins, scratch, flops, nbytes, *operands, sides=0):
    single = not isinstance(outs, tuple)
    return pl.pallas_call(
        kernel,
        out_shape=outs,
        in_specs=ins,
        out_specs=VMEM if single else (VMEM,) * (len(outs) - sides) + (ANY,) * sides,
        scratch_shapes=scratch,
        cost_estimate=pl.CostEstimate(flops=flops, bytes_accessed=nbytes, transcendentals=0),
    )(*operands)


def exchange(values):
    return lax.all_to_all(values, ("x", "z"), 0, 0)


def halo(bottom, top):
    count = 64
    forward = [(i, i + 1) for i in range(count - 1)]
    backward = [(target, source) for source, target in forward]
    return lax.ppermute(top, CLUS, forward), lax.ppermute(bottom, CLUS, backward)


def operator_twice(density, near_list, far_list, near_blocks, basis, transfer, coupling):
    share = array(SHARES, ROWS, 128)
    spread_out = array(PLANE, 32, 128)
    near_scratch = pltpu.VMEM((LEAVES, SHARES, NEAR_K * ROWS, PANEL), BF)
    vec_scratch = pltpu.VMEM((LEAVES + 2 * NWIN, PANEL, COLS), BF)
    rhs_scratch = pltpu.VMEM((HALF, 128), BF)
    near_sems = pltpu.SemaphoreType.DMA((LEAVES,))

    mine = call(
        stack_kernel, array(HELD, PANEL), [VMEM] * 3, [], 0, 1_400_000,
        near_blocks, basis, jnp.swapaxes(coupling, 2, 3),
    )
    held = lax.all_gather(mine, "y", axis=0)
    near_idx = near_list - (lax.axis_index(CLUS) * LEAVES - NWIN)
    near_idx = jnp.clip(near_idx, 0, LEAVES + 2 * NWIN - 1)
    sent = call(
        prepare_kernel, array(SHARES, SENT, 128), [VMEM] * 3, [], 40_000_000, 500_000,
        density, basis, transfer,
    )
    recv = lax.all_to_all(sent, "y", 0, 0)
    parents, bottom, top = call(
        parent_kernel, (spread_out, share, share), [VMEM], [], 100_000, 500_000, recv
    )
    every = lax.all_gather(exchange(parents), "core", axis=0)
    low, high = halo(bottom, top)
    first, parents, bottom, top, cpl, u = call(
        first_kernel,
        (
            array(SHARES, GROUPS, ROWS, 128), spread_out, share, share,
            array(2, 2 * RANK, HALF), array(GROUPS, PANEL, PACK * RANK),
        ),
        [SMEM, SMEM] + [ANY] * 3 + [VMEM] * 3,
        [
            near_scratch,
            pltpu.VMEM((SHARES, HELD - BAS0, 128), BF),
            pltpu.VMEM((FAR_K, RANK, 128), F32),
            rhs_scratch,
            vec_scratch,
            pltpu.VMEM((2, 2 * RANK, HALF), BF),
            pltpu.VMEM((GROUPS, PANEL, PACK * RANK), BF),
            pltpu.VMEM((2, PLANE, 32, 128), BF),
            pltpu.VMEM((LEAVES, RANK, RANK), BF),
            near_sems,
            pltpu.SemaphoreType.DMA,
            pltpu.SemaphoreType.DMA((2,)),
        ],
        400_000_000, 8_000_000,
        far_list, near_idx, every, held, transfer, recv, low, high,
        sides=2,
    )
    plane = exchange(parents)
    low, high = halo(bottom, top)
    near = call(
        near_kernel, array(GROUPS, PANEL, 128, dtype=F32), [SMEM, ANY] + [VMEM] * 3,
        [near_scratch, vec_scratch, near_sems], 300_000_000, 6_000_000,
        near_idx, held, first, low, high,
    )
    every = lax.all_gather(plane, "core", axis=0)
    sent = call(
        last_kernel, array(SHARES, 2, GROUPS, ROWS, 128), [SMEM] + [VMEM] * 5,
        [rhs_scratch], 100_000_000, 2_000_000,
        far_list, every, cpl, u, near, first,
    )
    out = array(LEAVES, ROWS, 256)
    return call(finish_kernel, (out, out), [VMEM], [], 0, 600_000, lax.all_to_all(sent, "y", 0, 0))


def solution(mesh):
    fine = Mesh(mesh.devices.reshape(4, 8, 2, 8), ("x", "z", "core", "y"))
    placed = (
        P(CLUS, "y", None),
        P(CLUS, None),
        P(CLUS, None),
        P(CLUS, None, "y", None),
        P(CLUS, "y", None),
        P(CLUS, None, None),
        P(CLUS, None, None, "y"),
    )
    return jax.shard_map(
        operator_twice,
        mesh=fine,
        in_specs=placed,
        out_specs=(P(CLUS, "y", None), P(CLUS, "y", None)),
        check_vma=False,
    )
```

```python
import functools

import jax
import jax.numpy as jnp
from jax import lax
from jax.experimental import pallas as pl
from jax.experimental.pallas import tpu as pltpu
from jax.sharding import Mesh
from jax.sharding import PartitionSpec as P

BF = jnp.bfloat16
F32 = jnp.float32
LEAVES = 16
ROWS = 16
PANEL = 128
RANK = 64
COLS = 32
PACK = 4
GROUPS = LEAVES // PACK
NEAR_K = 9
FAR_K = 27
NWIN = 4
SHARES = 8
PLANE = 32
PAR0 = GROUPS * ROWS
SENT = PAR0 + 32
BAS0 = LEAVES * NEAR_K * ROWS
CPL0 = BAS0 + LEAVES // 2 * ROWS
HELD = CPL0 + FAR_K * 8
HALF = FAR_K * 32
CHUNKS = 4
BATCH = 8
CLUS = ("x", "z", "core")
TOP = (((0,), (0,)), ((), ()))
ANY = pl.BlockSpec(memory_space=pl.ANY)
SMEM = pl.BlockSpec(memory_space=pltpu.SMEM)
VMEM = pl.BlockSpec(memory_space=pltpu.VMEM)


def dot(a, b):
    return jnp.dot(a, b, preferred_element_type=F32)


def dot_top(a, b):
    return lax.dot_general(a, b, TOP, preferred_element_type=F32)


def lane_group(shape):
    return lax.broadcasted_iota(jnp.int32, shape, len(shape) - 1) // COLS


def spread(rows):
    rows = rows + pltpu.roll(rows, 64, 1)
    return rows + pltpu.roll(rows, 32, 1)


def pack_parents(first, second):
    group = lane_group((32, 128))
    low = jnp.where(group == 0, first[:32], first[32:])
    high = jnp.where(group == 2, second[:32], second[32:])
    return jnp.where(group < 2, low, high).astype(BF)


def fetch(pairs, sems):
    moves = [pltpu.make_async_copy(src, dst, sems.at[n]) for n, (src, dst) in enumerate(pairs)]
    for move in moves:
        move.start()
    return moves


def stack_kernel(near_ref, b_ref, c_ref, out_ref, near_scr, rest_scr, sems, out_sems):
    size = BAS0 // CHUNKS
    moves = fetch([(near_ref.at[pl.ds(size * n, size)], near_scr.at[n]) for n in range(CHUNKS)], sems)
    for m in range(LEAVES // 2):
        rest_scr[ROWS * m : ROWS * (m + 1)] = jnp.concatenate([b_ref[2 * m], b_ref[2 * m + 1]], axis=1)
    both = jnp.concatenate([c_ref[0].astype(F32), c_ref[1].astype(F32)], axis=2)
    rest_scr[CPL0 - BAS0 :] = both.reshape(FAR_K * 8, 128).astype(BF)
    sends = [
        pltpu.make_async_copy(near_scr.at[n], out_ref.at[pl.ds(size * n, size)], out_sems.at[n])
        for n in range(CHUNKS)
    ]
    sends.append(pltpu.make_async_copy(rest_scr, out_ref.at[pl.ds(BAS0, HELD - BAS0)], out_sems.at[CHUNKS]))
    sends[CHUNKS].start()
    for n in range(CHUNKS):
        moves[n].wait()
        sends[n].start()
    for send in sends:
        send.wait()


def prepare_kernel(d_ref, b_ref, t_ref, out_ref):
    part = []
    for p in range(2):
        u = [dot(b_ref[i], t_ref[i]) for i in range(8 * p, 8 * p + 8)]
        rows = jnp.concatenate(u, axis=0).astype(BF)
        part.append(dot_top(rows, d_ref[8 * p : 8 * p + 8].reshape(8 * ROWS, 256)))
    for s in range(SHARES):
        cut = slice(COLS * s, COLS * (s + 1))
        pieces = [part[0][:32, cut], part[0][32:, cut], part[1][:32, cut], part[1][32:, cut]]
        out_ref[s, PAR0:SENT, :] = jnp.concatenate(pieces, axis=1).astype(BF)
        for g in range(GROUPS):
            pieces = [d_ref[PACK * g + l][:, cut] for l in range(PACK)]
            out_ref[s, ROWS * g : ROWS * (g + 1), :] = jnp.concatenate(pieces, axis=1)


def parent_kernel(recv_ref, out_ref, bottom_ref, top_ref):
    total = jnp.sum(recv_ref[:, PAR0:SENT, :].astype(F32), axis=0).astype(BF)
    out_ref[...] = jnp.broadcast_to(total[None], out_ref.shape)
    bottom_ref[...] = recv_ref[:, :ROWS, :]
    top_ref[...] = recv_ref[:, PAR0 - ROWS : PAR0, :]


def far_sums(far_ref, pc_ref, cpl, rhs_scr):
    side = lax.broadcasted_iota(jnp.int32, (32, 128), 1) // 64
    even = lane_group((RANK, 128)) % 2 == 0
    sums = []
    for p in range(2):
        for k in range(FAR_K):
            parent = far_ref[p, k]
            tile = pc_ref[(parent // 2) % 2, parent // 4]
            rhs_scr[32 * k : 32 * (k + 1), :] = jnp.where(side == parent % 2, tile, jnp.zeros_like(tile))
        rhs = rhs_scr[...]
        rows = slice(RANK * p, RANK * (p + 1))
        acc = dot(jnp.concatenate([cpl[0][rows], cpl[1][rows]], axis=0), rhs)
        sums.append(spread(jnp.where(even, acc[:RANK], acc[RANK:])).astype(BF).astype(F32))
    return sums


def far_field(u, coef):
    group = lane_group((RANK, 128))
    blocks = [jnp.where(group == l, coef, 0.0) for l in range(PACK)]
    return dot(u, jnp.concatenate(blocks, axis=0).astype(BF))


def near_copies(w_ref, near_scr, sems, leaves):
    size = NEAR_K * ROWS
    return [
        pltpu.make_async_copy(w_ref.at[:, pl.ds(size * i, size), :], near_scr.at[n], sems.at[n])
        for n, i in enumerate(leaves)
    ]


def unpack(start, tiles, v_scr):
    for n, tile in enumerate(tiles):
        for l in range(PACK):
            v_scr[PACK * (start + n) + l] = tile[:, COLS * l : COLS * (l + 1)]


def near_field(idx_ref, copies, near_scr, v_scr, leaves=range(LEAVES), batch=BATCH):
    for start in range(0, len(leaves), batch):
        for n in range(start, start + batch):
            copies[n].wait()
        cols = []
        for n in range(start, start + batch):
            parts = [near_scr[n, :, ROWS * k : ROWS * (k + 1), :].reshape(PANEL, PANEL) for k in range(NEAR_K)]
            rhs = jnp.concatenate([v_scr[idx_ref[leaves[n], k]] for k in range(NEAR_K)], axis=0)
            cols.append(dot(jnp.concatenate(parts, axis=1), rhs))
        for n in range(0, batch, PACK):
            yield jnp.concatenate(cols[n : n + PACK], axis=1)


def first_kernel(
    far_ref, idx_ref, pc_in, w_ref, t_in, recv_ref, lo_ref, hi_ref,
    out_ref, par_ref, bottom_ref, top_ref, cpl_out, u_out,
    near_scr, own_scr, c_scr, rhs_scr, v_scr, cpl_ref, u_ref, pc_ref, t_ref, sems, own_sem, side_sems,
):
    own = pltpu.make_async_copy(w_ref.at[:, pl.ds(BAS0, HELD - BAS0), :], own_scr, own_sem)
    own.start()
    sources = fetch(((t_in, t_ref), (pc_in, pc_ref)), side_sems)
    copies = near_copies(w_ref, near_scr, sems, range(LEAVES))
    tiles = [lo_ref[...]] + [recv_ref[:, ROWS * g : ROWS * (g + 1), :] for g in range(GROUPS)] + [hi_ref[...]]
    unpack(0, [tile.reshape(PANEL, 128) for tile in tiles], v_scr)
    own.wait()
    for source in sources:
        source.wait()
    for copy in copies[:BATCH]:
        copy.start()
    for y in range(SHARES):
        rows = own_scr[y, CPL0 - BAS0 :, :].astype(F32).reshape(FAR_K, 8, 128)
        c_scr[:, 8 * y : 8 * y + 8, :] = rows
    cpl = [c_scr[:, 32 * h : 32 * (h + 1), :].reshape(HALF, 128).T.astype(BF) for h in range(2)]
    for h in range(2):
        cpl_ref[h] = cpl[h]
    zero = jnp.zeros((RANK, RANK), BF)
    for m in range(LEAVES // 2):
        rows = own_scr[:, ROWS * m : ROWS * (m + 1), :].reshape(PANEL, 128)
        upper = jnp.concatenate([t_ref[2 * m], zero], axis=1)
        lower = jnp.concatenate([zero, t_ref[2 * m + 1]], axis=1)
        pair = dot(rows, jnp.concatenate([upper, lower], axis=0)).astype(BF)
        u_ref[m // 2, :, 128 * (m % 2) : 128 * (m % 2 + 1)] = pair
    for copy in copies[BATCH:]:
        copy.start()
    sides = fetch(((cpl_ref, cpl_out), (u_ref, u_out)), side_sems)
    coef = far_sums(far_ref, pc_ref, cpl, rhs_scr)
    group = lane_group((RANK, 128))
    parents = [jnp.zeros((RANK, 128), F32), jnp.zeros((RANK, 128), F32)]
    for g, near in enumerate(near_field(idx_ref, copies, near_scr, v_scr)):
        u = u_ref[g]
        res = (near + far_field(u, coef[g // 2])).astype(BF)
        tile = res.reshape(SHARES, ROWS, 128)
        out_ref[:, g] = tile
        if g == 0:
            bottom_ref[...] = tile
        if g == GROUPS - 1:
            top_ref[...] = tile
        x = dot_top(u, res)
        for l in range(PACK):
            parents[g // 2] += jnp.where(group == l, x[RANK * l : RANK * (l + 1)], 0.0)
    packed = pack_parents(spread(parents[0]), spread(parents[1]))
    par_ref[...] = jnp.broadcast_to(packed[None], par_ref.shape)
    for side in sides:
        side.wait()


def near_kernel(groups, idx_ref, w_ref, vec_ref, *refs):
    *ends, out_ref, near_scr, v_scr, sems = refs
    leaves = [i for g in groups for i in range(PACK * g, PACK * (g + 1))]
    copies = near_copies(w_ref, near_scr, sems, leaves)
    for copy in copies:
        copy.start()
    tiles = [vec_ref[:, g] for g in range(GROUPS)]
    unpack(1, [tile.reshape(PANEL, 128) for tile in tiles], v_scr)
    for start, ref in zip((0, GROUPS + 1), ends):
        unpack(start, [ref[...].reshape(PANEL, 128)], v_scr)
    for n, near in enumerate(near_field(idx_ref, copies, near_scr, v_scr, leaves, PACK)):
        out_ref[n] = near


def last_kernel(far_ref, pc_ref, cpl_ref, u_ref, mid_ref, edge_ref, own_ref, out_ref, rhs_scr):
    coef = far_sums(far_ref, pc_ref, (cpl_ref[0], cpl_ref[1]), rhs_scr)
    for g in range(GROUPS):
        near = mid_ref[g - 1] if 0 < g < GROUPS - 1 else edge_ref[g // (GROUPS - 1)]
        res = (near + far_field(u_ref[g], coef[g // 2])).astype(BF)
        out_ref[:, 0, g] = own_ref[:, g]
        out_ref[:, 1, g] = res.reshape(SHARES, ROWS, 128)


def finish_kernel(recv_ref, first_ref, second_ref):
    for o, ref in enumerate((first_ref, second_ref)):
        for g in range(GROUPS):
            for b in range(2):
                tiles = [recv_ref[PACK * b + s, o, g] for s in range(PACK)]
                for l in range(PACK):
                    cut = slice(COLS * l, COLS * (l + 1))
                    ref[PACK * g + l, :, 128 * b : 128 * (b + 1)] = jnp.concatenate([t[:, cut] for t in tiles], axis=1)


def array(*shape, dtype=BF):
    return jax.ShapeDtypeStruct(shape, dtype)


def call(kernel, outs, ins, scratch, flops, nbytes, *operands, sides=0):
    single = not isinstance(outs, tuple)
    return pl.pallas_call(
        kernel,
        out_shape=outs,
        in_specs=ins,
        out_specs=VMEM if single else (VMEM,) * (len(outs) - sides) + (ANY,) * sides,
        scratch_shapes=scratch,
        cost_estimate=pl.CostEstimate(flops=flops, bytes_accessed=nbytes, transcendentals=0),
    )(*operands)


def exchange(values):
    return lax.all_to_all(values, ("x", "z"), 0, 0)


def halo(bottom, top):
    count = 64
    forward = [(i, i + 1) for i in range(count - 1)]
    backward = [(target, source) for source, target in forward]
    return lax.ppermute(top, CLUS, forward), lax.ppermute(bottom, CLUS, backward)


def operator_twice(density, near_list, far_list, near_blocks, basis, transfer, coupling):
    share = array(SHARES, ROWS, 128)
    spread_out = array(PLANE, 32, 128)
    near_scratch = pltpu.VMEM((LEAVES, SHARES, NEAR_K * ROWS, PANEL), BF)
    vec_scratch = pltpu.VMEM((LEAVES + 2 * NWIN, PANEL, COLS), BF)
    rhs_scratch = pltpu.VMEM((HALF, 128), BF)
    near_sems = pltpu.SemaphoreType.DMA((LEAVES,))

    mine = call(
        stack_kernel, (array(HELD, PANEL),), [ANY] + [VMEM] * 2,
        [
            pltpu.VMEM((CHUNKS, BAS0 // CHUNKS, PANEL), BF),
            pltpu.VMEM((HELD - BAS0, PANEL), BF),
            pltpu.SemaphoreType.DMA((CHUNKS,)),
            pltpu.SemaphoreType.DMA((CHUNKS + 1,)),
        ],
        0, 1_400_000,
        near_blocks.reshape(BAS0, PANEL), basis, jnp.swapaxes(coupling, 2, 3),
        sides=1,
    )[0]
    held = lax.all_gather(mine, "y", axis=0)
    near_idx = near_list - (lax.axis_index(CLUS) * LEAVES - NWIN)
    near_idx = jnp.clip(near_idx, 0, LEAVES + 2 * NWIN - 1)
    sent = call(
        prepare_kernel, array(SHARES, SENT, 128), [VMEM] * 3, [], 40_000_000, 500_000,
        density, basis, transfer,
    )
    recv = lax.all_to_all(sent, "y", 0, 0)
    parents, bottom, top = call(parent_kernel, (spread_out, share, share), [VMEM], [], 100_000, 500_000, recv)
    every = lax.all_gather(exchange(parents), "core", axis=0)
    low, high = halo(bottom, top)
    first, parents, bottom, top, cpl, u = call(
        first_kernel,
        (
            array(SHARES, GROUPS, ROWS, 128), spread_out, share, share,
            array(2, 2 * RANK, HALF), array(GROUPS, PANEL, PACK * RANK),
        ),
        [SMEM, SMEM] + [ANY] * 3 + [VMEM] * 3,
        [
            near_scratch,
            pltpu.VMEM((SHARES, HELD - BAS0, 128), BF),
            pltpu.VMEM((FAR_K, RANK, 128), F32),
            rhs_scratch,
            vec_scratch,
            pltpu.VMEM((2, 2 * RANK, HALF), BF),
            pltpu.VMEM((GROUPS, PANEL, PACK * RANK), BF),
            pltpu.VMEM((2, PLANE, 32, 128), BF),
            pltpu.VMEM((LEAVES, RANK, RANK), BF),
            near_sems,
            pltpu.SemaphoreType.DMA,
            pltpu.SemaphoreType.DMA((2,)),
        ],
        400_000_000, 8_000_000,
        far_list, near_idx, every, held, transfer, recv, low, high,
        sides=2,
    )
    plane = exchange(parents)
    low, high = halo(bottom, top)
    half = array(GROUPS // 2, PANEL, 128, dtype=F32)
    half_scratch = [
        pltpu.VMEM((LEAVES // 2, SHARES, NEAR_K * ROWS, PANEL), BF),
        vec_scratch,
        pltpu.SemaphoreType.DMA((LEAVES // 2,)),
    ]
    mid = call(
        functools.partial(near_kernel, (1, 2)), half, [SMEM, ANY, VMEM],
        half_scratch, 150_000_000, 3_000_000,
        near_idx, held, first,
    )
    edge = call(
        functools.partial(near_kernel, (0, 3)), half, [SMEM, ANY] + [VMEM] * 3,
        half_scratch, 150_000_000, 3_000_000,
        near_idx, held, first, low, high,
    )
    every = lax.all_gather(plane, "core", axis=0)
    sent = call(
        last_kernel, array(SHARES, 2, GROUPS, ROWS, 128), [SMEM] + [VMEM] * 6,
        [rhs_scratch], 100_000_000, 2_000_000,
        far_list, every, cpl, u, mid, edge, first,
    )
    out = array(LEAVES, ROWS, 256)
    return call(finish_kernel, (out, out), [VMEM], [], 0, 600_000, lax.all_to_all(sent, "y", 0, 0))


def solution(mesh):
    fine = Mesh(mesh.devices.reshape(4, 8, 2, 8), ("x", "z", "core", "y"))
    placed = (
        P(CLUS, "y", None),
        P(CLUS, None),
        P(CLUS, None),
        P(CLUS, None, "y", None),
        P(CLUS, "y", None),
        P(CLUS, None, None),
        P(CLUS, None, None, "y"),
    )
    return jax.shard_map(
        operator_twice,
        mesh=fine,
        in_specs=placed,
        out_specs=(P(CLUS, "y", None), P(CLUS, "y", None)),
        check_vma=False,
    )
```
